1024 devices in a mesh: ctx: 256 (over y_hi, x, z), tp: 4 (over y_lo, core).
Axes of the slice: x: 4, y: 4 (y_hi: 2, y_lo: 2; y = y_hi * 2 + y_lo), z: 32, core: 2. Of those that a mesh axis runs over, the one named last changes fastest.
Arguments:
- hyena_q: bfloat16 [65536, 4096], P('ctx', 'tp'), may hold values from -6 to 6
- hyena_k: bfloat16 [65536, 4096], P('ctx', 'tp'), may hold values from -6 to 6
- hyena_v: bfloat16 [65536, 4096], P('ctx', 'tp'), may hold values from -6 to 6
- filters: bfloat16 [256, 128], P('tp'), may hold values from -0.5 to 0.5
- direct: bfloat16 [4096], P('tp'), may hold values from -4 to 4
- queries: bfloat16 [65536, 2048], P('ctx', 'tp'), may hold values from -64 to 64
- keys: bfloat16 [65536, 2048], P('ctx', 'tp'), may hold values from -4 to 4
- values: bfloat16 [65536, 2048], P('ctx', 'tp'), may hold values from -6 to 6
- segment_ids: int32 [65536], P('ctx'), may hold values from 0 to 127, never falling along the last dimension, each value on 1 to 1793 neighbouring positions
- out_weight: bfloat16 [2048, 4096], P(None, 'tp'), may hold values from -0.125 to 0.125
Outputs:
- hyena_out: bfloat16 [65536, 4096], P('ctx', 'tp')
- attn_out: bfloat16 [65536, 4096], P('ctx', 'tp')
The draws below stay inside these ranges and needn't reach their ends.
Inputs may be any that keep to these rules, and one draw needn't show every extreme that they name: `segment_ids`: ids never fall along the sequence; each document holds 1 to 1793 tokens and one holds exactly 1793.
All inputs are finite; a program needn't handle non-finite values.
Results may differ from the reference program's by a relative error of at most 0.006.
Values may be sent and summed in bfloat16 or wider, within the bound.
A program may use at most 64 MiB of HBM per device.

```python
import math
import jax
import jax.numpy as jnp
import numpy as np
from jax import lax

D = 4096
HD = 128
KERNEL = 128
GROUP = 16
HEADS = 16
TOK_DEV = 256
WINDOW = 8
TOKENS = 65536
FEAT = 2048
GROUPS = 256
MAXDOC = 1793
DOCS = 128
N_CTX = 256


def query_key_pair(key):
    base = jax.random.fold_in(key, 4242)
    shape = (TOKENS, FEAT)
    keys = jnp.clip(jax.random.normal(jax.random.fold_in(base, 1), shape, jnp.float32), -4.0, 4.0)
    queries = jnp.clip(2.0 * jax.random.normal(jax.random.fold_in(base, 2), shape, jnp.float32), -8.0, 8.0)
    return (queries, keys)


def draw_queries(key, part):
    return query_key_pair(key)[0].astype(jnp.bfloat16)


def draw_keys(key, part):
    return query_key_pair(key)[1].astype(jnp.bfloat16)


def levels(stream_key, dims, cuts, low, top_value):
    level, own = 1.0, jax.random.fold_in(stream_key, 6)
    for dim, blocks in cuts:
        heights = jnp.exp(jax.random.uniform(jax.random.fold_in(own, dim), (blocks,), jnp.float32, low / len(cuts), top_value / len(cuts)))
        level = level * jnp.repeat(heights, dims[dim] // blocks).reshape([-1 if axis == dim else 1 for axis in range(len(dims))])
    return level


def length_profile(amount, total, bound, skew):
    weights = [(1 << 20) // math.isqrt(standing ** skew) + 1 for standing in range(2, amount + 1)]
    surplus, given = total - bound - (amount - 1), [1] * (amount - 1)
    while surplus > 0:
        free = [i for i in range(amount - 1) if given[i] < bound]
        pool, budget = sum([weights[i] for i in free]), surplus
        for i in free:
            more = min(bound - given[i], max(1, budget * weights[i] // pool), surplus)
            given[i] = given[i] + more
            surplus = surplus - more
    return np.array([bound] + given)


def uneven(own_key, number_of, total, most, lean):
    if number_of == 2:
        one = jax.random.randint(own_key, (), max(1, total - most), min(most, total - 1) + 1)
        return jnp.stack([one, total - one])
    lengths = jnp.asarray(length_profile(number_of, total, most, lean), jnp.int32)
    pairs = (number_of - 1) // 2
    giver, sink = lengths[1:1 + 2 * pairs:2], lengths[2:2 + 2 * pairs:2]
    room = jnp.minimum(giver - 1, most - sink)
    passed = jax.random.randint(jax.random.fold_in(own_key, 1), (pairs,), 0, 1 << 20) % (room + 1)
    lengths = lengths.at[1:1 + 2 * pairs:2].set(giver - passed).at[2:2 + 2 * pairs:2].set(sink + passed)
    return lengths[jax.random.permutation(jax.random.fold_in(own_key, 2), number_of)]


def normal_values(rng, extent, scale, most, split=(), held_as=jnp.bfloat16):
    result = jax.random.normal(rng, extent, jnp.float32) * scale
    if len(split) > 0:
        result = levels(rng, extent, split, -0.22, 0.18) * result
    return jnp.clip(result, min=-most, max=most).astype(held_as)


def setup_inputs(seed: int = 0) -> dict:
    seeds = jax.random.split(jax.random.key(seed), 11)
    hyena_q = normal_values(seeds[0], (TOKENS, D), 1.0, 6.0, ((0, 256), (1, 4)))
    hyena_k = normal_values(seeds[1], (TOKENS, D), 1.0, 6.0, ((0, 256), (1, 4)))
    hyena_v = normal_values(seeds[2], (TOKENS, D), 1.0, 6.0, ((0, 256), (1, 4)))
    filters = normal_values(seeds[3], (GROUPS, KERNEL), KERNEL ** -0.5, 0.5, ((0, 4),))
    direct = normal_values(seeds[4], (D,), 1.0, 4.0, ((0, 4),))
    queries = draw_queries(jax.random.fold_in(seeds[10], 71), 0)
    keys = draw_keys(jax.random.fold_in(seeds[10], 71), 0)
    values = normal_values(seeds[7], (TOKENS, FEAT), 1.0, 6.0, ((0, 256), (1, 4)))
    segment_ids = jnp.searchsorted(jnp.cumsum(uneven(seeds[8], DOCS, TOKENS, MAXDOC, 2)), jnp.arange(TOKENS), side="right").astype(jnp.int32)
    out_weight = normal_values(seeds[9], (FEAT, D), FEAT ** -0.5, 0.125, ((1, 4),))
    return dict(hyena_q=hyena_q, hyena_k=hyena_k, hyena_v=hyena_v, filters=filters, direct=direct, queries=queries, keys=keys, values=values, segment_ids=segment_ids, out_weight=out_weight)


NEG = -1e+30

def toeplitz(filters, rows):
    kernel = filters.shape[1]
    span = rows + kernel - 1
    flipped = filters[:, ::-1].astype(jnp.float32)
    padded = jnp.concatenate([flipped, jnp.zeros((filters.shape[0], span + 1 - kernel), jnp.float32)], axis=1)
    tiled = jnp.tile(padded, (1, rows))[:, :rows * span]
    return tiled.reshape(filters.shape[0], rows, span)

def reference(hyena_q, hyena_k, hyena_v, filters, direct, queries, keys, values, segment_ids, out_weight):
    mixed = (hyena_k.astype(jnp.float32) * hyena_v.astype(jnp.float32)).astype(jnp.bfloat16)
    mixed = lax.optimization_barrier(mixed)
    table = toeplitz(filters, KERNEL)
    padded = jnp.concatenate([jnp.zeros((KERNEL - 1, D), jnp.bfloat16), mixed], axis=0)

    def conv_block(index):
        window = lax.dynamic_slice_in_dim(padded, (index * KERNEL).astype(jnp.int32), 2 * KERNEL - 1, 0)
        window = window.reshape(2 * KERNEL - 1, GROUPS, GROUP).astype(jnp.float32)
        return jnp.einsum('gts,sgc->tgc', table, window).reshape(KERNEL, D)
    conv = lax.map(conv_block, jnp.arange(TOKENS // KERNEL, dtype=jnp.int32)).reshape(TOKENS, D)
    hyena_out = (hyena_q.astype(jnp.float32) * (conv + direct.astype(jnp.float32) * mixed.astype(jnp.float32))).astype(jnp.bfloat16)
    reach = (WINDOW - 1) * TOK_DEV
    key_pad = jnp.concatenate([jnp.zeros((reach, FEAT), jnp.bfloat16), keys], axis=0)
    value_pad = jnp.concatenate([jnp.zeros((reach, FEAT), jnp.bfloat16), values], axis=0)
    seg_pad = jnp.concatenate([jnp.full((reach,), -1, jnp.int32), segment_ids], axis=0)
    query_pos = jnp.arange(TOK_DEV, dtype=jnp.int32) + reach
    key_pos = jnp.arange(WINDOW * TOK_DEV, dtype=jnp.int32)
    causal = key_pos[None, :] <= query_pos[:, None]

    def attend(index):
        start = (index * TOK_DEV).astype(jnp.int32)
        query_blk = lax.dynamic_slice_in_dim(queries, start, TOK_DEV, 0).reshape(TOK_DEV, HEADS, HD).astype(jnp.float32)
        key_blk = lax.dynamic_slice_in_dim(key_pad, start, WINDOW * TOK_DEV, 0).reshape(WINDOW * TOK_DEV, HEADS, HD).astype(jnp.float32)
        value_blk = lax.dynamic_slice_in_dim(value_pad, start, WINDOW * TOK_DEV, 0).reshape(WINDOW * TOK_DEV, HEADS, HD).astype(jnp.float32)
        query_seg = lax.dynamic_slice_in_dim(segment_ids, start, TOK_DEV, 0)
        key_seg = lax.dynamic_slice_in_dim(seg_pad, start, WINDOW * TOK_DEV, 0)
        allowed = (query_seg[:, None] == key_seg[None, :]) & causal
        score = jnp.einsum('qhd,khd->hqk', query_blk, key_blk) / jnp.sqrt(jnp.float32(HD))
        score = jnp.where(allowed[None], score, NEG)
        highest = lax.optimization_barrier(jnp.max(score, axis=-1, keepdims=True))
        expo = jnp.exp(score - highest)
        total = lax.optimization_barrier(jnp.sum(expo, axis=-1))
        weight = lax.optimization_barrier(expo.astype(jnp.bfloat16))
        summed = jnp.einsum('hqk,khd->qhd', weight.astype(jnp.float32), value_blk)
        return (summed / total.T[:, :, None]).reshape(TOK_DEV, FEAT).astype(jnp.bfloat16)
    attn = lax.map(attend, jnp.arange(N_CTX, dtype=jnp.int32)).reshape(TOKENS, FEAT)
    attn_out = jnp.dot(attn, out_weight, preferred_element_type=jnp.float32).astype(jnp.bfloat16)
    return (hyena_out, attn_out)
```

```python
import functools
import math

import jax
import jax.numpy as jnp
from jax import lax
from jax.experimental import pallas as pl
from jax.experimental.pallas import tpu as pltpu
from jax.sharding import PartitionSpec as P

HD = 128
WINDOW = 8
TAPS = 128
GROUP = 16
KEY_HOPS = 2
QUERY_HOPS = WINDOW - 1 - KEY_HOPS
NEG = -1e30
MESH = pl.DeviceIdType.MESH


def plan(heads, blocks):
    chunk, lag = 1.41, 1.9
    free = {"neg": 0.0, "pos": 0.0, "tp": 0.0, "mate": 0.0}
    ready = {}
    order = []
    todo = []

    def add(name, needs, cost, link=None, size=1.0, rank=0):
        todo.append(dict(name=name, needs=needs, cost=cost, link=link, size=size, rank=rank))

    for r in range(1, QUERY_HOPS + 1):
        for h in range(heads):
            add(("q", h, r), [("q", h, r - 1)] if r > 1 else [], 0.03, "neg", 1.0, r)
    for r in range(1, KEY_HOPS + 1):
        for h in range(heads):
            add(("k", h, r), [("k", h, r - 1)] if r > 1 else [], 0.03, "pos", 1.0, r)
        for h in range(heads):
            add(("v", h, r), [("v", h, r - 1)] if r > 1 else [("vt", h)], 0.03, "pos", 1.0, r)
    for h in range(heads):
        add(("vt", h), [], 0.15, rank=1)
        add(("halo", h), [("mix",), ("sent", "v", heads - 1, KEY_HOPS)], 0.03, "pos", 1.0, 5)
    add(("mix",), [], 1.0, rank=2)
    for d in range(KEY_HOPS + 1):
        add(("segk", d), [("q", 0, 1)] if d == 0 else [("k", 0, d)], 0.1, rank=3)
    for h in range(heads):
        for a in range(QUERY_HOPS, 0, -1):
            add(("part", h, a), [("q", h, a), ("k", h, KEY_HOPS), ("v", h, KEY_HOPS), ("segk", KEY_HOPS)], 0.4, rank=10 + (0 if a == QUERY_HOPS else 1))
        for d in range(KEY_HOPS + 1):
            need = [("k", h, d), ("v", h, d)] if d else [("vt", h)]
            add(("local", h, d), need + [("segk", d)] + ([("local", h, d - 1)] if d else []), 0.4, rank=20 + d)
        for a in range(QUERY_HOPS, 0, -1):
            need = [("part", h, a)] + ([("o", h, a + 1)] if a < QUERY_HOPS else [])
            add(("o", h, a), need, 0.2 if a < QUERY_HOPS else 0.05, "pos", 1.0, 4)
        add(("home", h), [("o", h, 1), ("local", h, KEY_HOPS)], 0.3, rank=5)
        add(("g0", h), [("home", h)], 0.03, "mate", 0.1, 6)
        add(("g1", h), [("home", h)], 0.03, "tp", 1.0, 5)
        add(("g2", h), [("g1", h)], 0.03, "mate", 0.1, 5)
    for p in range(heads // 2):
        for j, kind in enumerate(("home", "g0", "g1", "g2")):
            add(("proj", p, j), [(kind, 2 * p), (kind, 2 * p + 1)], 0.4, rank=30 + p * 4 + j)
    add(("taps",), [], 0.5, rank=40)
    for c in range(blocks):
        add(("hyena", c), [("taps",), ("mix",)] + [("halo", h) for h in range(heads)], 1.2, rank=50)

    now = 0.0
    while todo:
        best = None
        horizon = None
        for item in todo:
            when = 0.0
            for need in item["needs"]:
                when = max(when, ready.get(need, math.inf))
            if when <= now:
                if best is None or item["rank"] < best["rank"]:
                    best = item
            elif when < math.inf:
                horizon = when if horizon is None else min(horizon, when)
        if best is None:
            now = horizon
            continue
        todo.remove(best)
        order.append(best["name"])
        now += best["cost"]
        if best["link"]:
            begin = max(now, free[best["link"]])
            free[best["link"]] = begin + best["size"] * chunk
            ready[best["name"]] = free[best["link"]] + lag
            ready[("sent",) + best["name"]] = now
        else:
            ready[best["name"]] = now
    return order


def merge(first, second):
    high_a, total_a, sum_a = first
    high_b, total_b, sum_b = second
    high = jnp.maximum(high_a, high_b)
    fade_a, fade_b = jnp.exp2(high_a - high), jnp.exp2(high_b - high)
    return high, total_a * fade_a + total_b * fade_b, sum_a * fade_a + sum_b * fade_b


def kernel(
    heads,
    order,
    hq_hbm, hk_hbm, hv_hbm, filters_hbm, direct_hbm, q_hbm, k_hbm, v_hbm, seg_hbm, w_hbm,
    hyena_out, attn_out,
    hq, hk, hv, filters, direct, q_own, k_own, v_own, vt_own, seg_own, weight,
    q_in, segq_in, k_in, vt_in, segk_in, segk_col, ext, taps,
    part_sum, part_stat, out_sum, out_stat, in_sum, in_stat, local_sum, local_stat,
    attn, attn_in, total,
    load_sem, head_sem, q_sem, k_sem, v_sem, segq_sem, segk_sem, halo_sem, o_sem, ostat_sem, g_sem,
):
    ctx, tp = lax.axis_index("ctx"), lax.axis_index("tp")
    count = lax.axis_size("ctx")
    right, left = lax.rem(ctx + 1, count), lax.rem(ctx + count - 1, count)
    mate = tp + 1 - 2 * lax.rem(tp, 2)
    across = lax.rem(tp + 2, 4)
    diagonal = lax.rem(mate + 2, 4)
    rows, chans = hk.shape
    scale = math.log2(math.e) / math.sqrt(HD)

    loads = {}

    def load(name, source, target, sem):
        loads[name] = pltpu.make_async_copy(source, target, sem)
        loads[name].start()

    for h in range(heads):
        load(("q", h), q_hbm.at[:, pl.ds(h * HD, HD)], q_own.at[h], head_sem.at[0, h])
        load(("k", h), k_hbm.at[:, pl.ds(h * HD, HD)], k_own.at[h], head_sem.at[1, h])
        load(("v", h), v_hbm.at[:, pl.ds(h * HD, HD)], v_own.at[h], head_sem.at[2, h])
    load("seg", seg_hbm, seg_own, load_sem.at[0])
    load("hk", hk_hbm, hk, load_sem.at[1])
    load("hv", hv_hbm, hv, load_sem.at[2])
    load("filters", filters_hbm, filters, load_sem.at[3])
    load("direct", direct_hbm, direct, load_sem.at[4])
    load("hq", hq_hbm, hq, load_sem.at[5])
    load("weight", w_hbm, weight, load_sem.at[6])

    done = set()

    def loaded(name):
        if name not in done:
            done.add(name)
            loads[name].wait()

    barrier = pltpu.get_barrier_semaphore()
    for peer in ({"ctx": left}, {"ctx": right}, {"tp": mate}, {"tp": across}):
        pl.semaphore_signal(barrier, inc=1, device_id=peer, device_id_type=MESH)
    pl.semaphore_wait(barrier, 4)

    copies = {}

    def copy(name, source, target, sems, index, peer):
        copies[name] = pltpu.make_async_remote_copy(
            src_ref=source,
            dst_ref=target,
            send_sem=sems.at[(0,) + index],
            recv_sem=sems.at[(1,) + index],
            device_id=peer,
            device_id_type=MESH,
        )

    for r in range(1, QUERY_HOPS + 1):
        for h in range(heads):
            copy(("q", h, r), q_own.at[h] if r == 1 else q_in.at[r - 2, h], q_in.at[r - 1, h], q_sem, (r - 1, h), {"ctx": left})
            copy(("o", h, r), out_sum.at[r - 1, h], in_sum.at[r - 1, h], o_sem, (r - 1, h), {"ctx": right})
            copy(("ostat", h, r), out_stat.at[r - 1, h], in_stat.at[r - 1, h], ostat_sem, (r - 1, h), {"ctx": right})
        copy(("segq", r), seg_own if r == 1 else segq_in.at[r - 2], segq_in.at[r - 1], segq_sem, (r - 1,), {"ctx": left})
    for r in range(1, KEY_HOPS + 1):
        for h in range(heads):
            copy(("k", h, r), k_own.at[h] if r == 1 else k_in.at[r - 2, h], k_in.at[r - 1, h], k_sem, (r - 1, h), {"ctx": right})
            copy(("v", h, r), vt_own.at[h] if r == 1 else vt_in.at[r - 2, h], vt_in.at[r - 1, h], v_sem, (r - 1, h), {"ctx": right})
        copy(("segk", r), seg_own if r == 1 else segk_in.at[r - 2], segk_in.at[r - 1], segk_sem, (r - 1,), {"ctx": right})
    strip = chans // heads
    for h in range(heads):
        lanes = pl.ds(h * strip, strip)
        copy(("halo", h), ext.at[pl.ds(rows, TAPS), lanes], ext.at[pl.ds(0, TAPS), lanes], halo_sem, (h,), {"ctx": right})
        half = pl.ds(h % 2 * HD, HD)
        mine = attn.at[h // 2, :, half]
        copy(("g0", h), mine, attn_in.at[0, h // 2, :, half], g_sem, (0, h), {"tp": mate})
        copy(("g1", h), mine, attn_in.at[1, h // 2, :, half], g_sem, (1, h), {"tp": across})
        copy(("g2", h), attn_in.at[1, h // 2, :, half], attn_in.at[2, h // 2, :, half], g_sem, (2, h), {"tp": mate})

    got = set()

    def arrived(name):
        if name not in got:
            got.add(name)
            copies[name].wait_recv()

    def send(name):
        copies[name].start()

    def column(row):
        return jnp.transpose(jnp.broadcast_to(row.astype(jnp.float32), (HD, rows)))

    def partial(query, query_seg, key, value_t, key_col, causal):
        score = lax.dot_general(key[...], query[...], (((1,), (1,)), ((), ())), preferred_element_type=jnp.float32)
        col = key_col[...]
        allowed = jnp.concatenate([col] * (rows // HD), axis=1) == query_seg[...].astype(jnp.float32)
        if causal:
            allowed = allowed & (
                lax.broadcasted_iota(jnp.int32, (rows, rows), 0) <= lax.broadcasted_iota(jnp.int32, (rows, rows), 1)
            )
        score = jnp.where(allowed, score * scale, NEG)
        high = jnp.max(score, axis=0, keepdims=True)
        expo = jnp.exp2(score - high)
        amount = jnp.sum(expo, axis=0, keepdims=True)
        summed = jnp.dot(value_t[...], expo.astype(jnp.bfloat16), preferred_element_type=jnp.float32)
        return high, amount, summed

    def keep(state, stat_ref, sum_ref):
        stat_ref[0:1, :] = state[0]
        stat_ref[1:2, :] = state[1]
        sum_ref[...] = state[2].astype(sum_ref.dtype)

    def fetch(stat_ref, sum_ref):
        return stat_ref[0:1, :], stat_ref[1:2, :], sum_ref[...].astype(jnp.float32)

    def step_q(h, r):
        if r == 1:
            loaded(("q", h))
            if h == 0:
                loaded("seg")
        else:
            arrived(("q", h, r - 1))
            if h == 0:
                arrived(("segq", r - 1))
        if h == 0:
            send(("segq", r))
        send(("q", h, r))

    def step_k(h, r):
        if r == 1:
            loaded(("k", h))
            if h == 0:
                loaded("seg")
        else:
            arrived(("k", h, r - 1))
            if h == 0:
                arrived(("segk", r - 1))
        if h == 0:
            send(("segk", r))
        send(("k", h, r))

    def step_vt(h):
        loaded(("v", h))
        vt_own[h] = jnp.transpose(v_own[h])

    def step_v(h, r):
        if r > 1:
            arrived(("v", h, r - 1))
        send(("v", h, r))

    def step_mix():
        loaded("hk")
        loaded("hv")
        for lo in range(0, rows, 64):
            ext[pl.ds(TAPS + lo, 64), :] = (
                hk[pl.ds(lo, 64), :].astype(jnp.float32) * hv[pl.ds(lo, 64), :].astype(jnp.float32)
            ).astype(jnp.bfloat16)

    def step_halo(h):
        send(("halo", h))

    def step_segk(d):
        if d == 0:
            loaded("seg")
            segk_col[0] = column(seg_own[...])
        else:
            arrived(("segk", d))
            segk_col[d] = column(segk_in[d - 1])

    def step_part(h, a):
        arrived(("q", h, a))
        arrived(("segq", a))
        arrived(("k", h, KEY_HOPS))
        arrived(("v", h, KEY_HOPS))
        state = partial(q_in.at[a - 1, h], segq_in.at[a - 1], k_in.at[KEY_HOPS - 1, h], vt_in.at[KEY_HOPS - 1, h], segk_col.at[KEY_HOPS], False)
        if a == QUERY_HOPS:
            keep(state, out_stat.at[a - 1, h], out_sum.at[a - 1, h])
        else:
            keep(state, part_stat.at[a - 1, h], part_sum.at[a - 1, h])

    def step_local(h, d):
        if d == 0:
            state = partial(q_own.at[h], seg_own, k_own.at[h], vt_own.at[h], segk_col.at[0], True)
        else:
            arrived(("k", h, d))
            arrived(("v", h, d))
            state = partial(q_own.at[h], seg_own, k_in.at[d - 1, h], vt_in.at[d - 1, h], segk_col.at[d], False)
            state = merge(fetch(local_stat.at[h], local_sum.at[h]), state)
        keep(state, local_stat.at[h], local_sum.at[h])

    def step_o(h, a):
        if a < QUERY_HOPS:
            arrived(("o", h, a + 1))
            arrived(("ostat", h, a + 1))
            state = merge(fetch(part_stat.at[a - 1, h], part_sum.at[a - 1, h]), fetch(in_stat.at[a, h], in_sum.at[a, h]))
            keep(state, out_stat.at[a - 1, h], out_sum.at[a - 1, h])
        send(("o", h, a))
        send(("ostat", h, a))

    def step_home(h):
        arrived(("o", h, 1))
        arrived(("ostat", h, 1))
        _, amount, summed = merge(fetch(local_stat.at[h], local_sum.at[h]), fetch(in_stat.at[0, h], in_sum.at[0, h]))
        result = jnp.transpose(summed / amount)
        attn[h // 2, :, pl.ds(h % 2 * HD, HD)] = result.astype(jnp.bfloat16)

    def step_g0(h):
        send(("g0", h))

    def step_g1(h):
        send(("g1", h))

    def step_g2(h):
        arrived(("g1", h))
        send(("g2", h))

    projected = []
    width = 256

    def step_proj(p, j):
        loaded("weight")
        if j:
            for h in (2 * p, 2 * p + 1):
                arrived((("g0", "g1", "g2")[j - 1], h))
        block = attn[p] if j == 0 else attn_in[j - 1, p]
        owner = (tp, mate, across, diagonal)[j]
        start = pl.multiple_of(owner * (heads * HD) + p * 2 * HD, 2 * HD)
        first, last = not projected, len(projected) == 2 * heads - 1
        projected.append((p, j))
        for lo in range(0, chans, width):
            lanes = pl.ds(lo, width)
            term = jnp.dot(block, weight[pl.ds(start, 2 * HD), lanes], preferred_element_type=jnp.float32)
            if not first:
                term = total[:, lanes] + term
            if last:
                attn_out[:, lanes] = term.astype(jnp.bfloat16)
            else:
                total[:, lanes] = term

    def step_taps():
        loaded("filters")
        tap = lax.broadcasted_iota(jnp.int32, (TAPS, 2 * TAPS), 0)
        place = lax.broadcasted_iota(jnp.int32, (TAPS, 2 * TAPS), 1)
        flip = jnp.where(tap + place == TAPS, 1.0, 0.0).astype(jnp.bfloat16)
        taps[...] = jnp.dot(filters[...], flip, preferred_element_type=jnp.float32)

    def step_hyena(c):
        if c == 0:
            for h in range(heads):
                arrived(("halo", h))
            loaded("hq")
            loaded("direct")
        lanes = pl.ds(c * 128, 128)
        before = ext[pl.ds(0, TAPS), lanes]
        before = jnp.where(ctx == 0, jnp.zeros_like(before), before)
        upper, lower = ext[pl.ds(TAPS, TAPS), lanes], ext[pl.ds(2 * TAPS, TAPS), lanes]
        data = jnp.concatenate(
            [jnp.concatenate([before, upper], axis=0), jnp.concatenate([upper, lower], axis=0)], axis=1
        )
        group = lax.rem(lax.broadcasted_iota(jnp.int32, (TAPS, 2 * TAPS), 1), 128) // GROUP
        conv = jnp.zeros((TAPS, 2 * TAPS), jnp.float32)
        per = 128 // GROUP
        for g in range(per):
            row = jnp.broadcast_to(taps[pl.ds(c * per + g, 1), :], (TAPS, 2 * TAPS))
            table = pltpu.roll(row, 0, 1, stride=1, stride_axis=0).astype(jnp.bfloat16)
            conv = jnp.where(group == g, jnp.dot(table, data, preferred_element_type=jnp.float32), conv)
        gain = direct[:, lanes].astype(jnp.float32)
        for b, mixed in enumerate((upper, lower)):
            span = pl.ds(b * TAPS, TAPS)
            hyena_out[span, lanes] = (
                hq[span, lanes].astype(jnp.float32)
                * (conv[:, b * TAPS : (b + 1) * TAPS] + gain * mixed.astype(jnp.float32))
            ).astype(jnp.bfloat16)

    steps = dict(
        q=step_q, k=step_k, vt=step_vt, v=step_v, mix=step_mix, halo=step_halo, segk=step_segk, part=step_part,
        local=step_local, o=step_o, home=step_home, g0=step_g0, g1=step_g1, g2=step_g2, proj=step_proj,
        taps=step_taps, hyena=step_hyena,
    )
    for name in order:
        steps[name[0]](*name[1:])
    for name in copies:
        arrived(name)
        copies[name].wait_send()


def local(hyena_q, hyena_k, hyena_v, filters, direct, queries, keys, values, segment_ids, out_weight):
    rows, feat = queries.shape
    chans = hyena_k.shape[1]
    heads = feat // HD
    groups = filters.shape[0]
    depth = out_weight.shape[0]
    bf16, f32, i32 = jnp.bfloat16, jnp.float32, jnp.int32
    dma = pltpu.SemaphoreType.DMA
    vmem = pltpu.VMEM
    scratch = [
        vmem((rows, chans), bf16), vmem((rows, chans), bf16), vmem((rows, chans), bf16),
        vmem((groups, TAPS), bf16), vmem((1, chans), bf16),
        vmem((heads, rows, HD), bf16), vmem((heads, rows, HD), bf16), vmem((heads, rows, HD), bf16),
        vmem((heads, HD, rows), bf16), vmem((1, rows), i32), vmem((depth, chans), bf16),
        vmem((QUERY_HOPS, heads, rows, HD), bf16), vmem((QUERY_HOPS, 1, rows), i32),
        vmem((KEY_HOPS, heads, rows, HD), bf16), vmem((KEY_HOPS, heads, HD, rows), bf16), vmem((KEY_HOPS, 1, rows), i32),
        vmem((KEY_HOPS + 1, rows, HD), f32), vmem((TAPS + rows, chans), bf16), vmem((groups, 2 * TAPS), f32),
        vmem((QUERY_HOPS, heads, HD, rows), f32), vmem((QUERY_HOPS, heads, 2, rows), f32),
        vmem((QUERY_HOPS, heads, HD, rows), bf16), vmem((QUERY_HOPS, heads, 2, rows), f32),
        vmem((QUERY_HOPS, heads, HD, rows), bf16), vmem((QUERY_HOPS, heads, 2, rows), f32),
        vmem((heads, HD, rows), f32), vmem((heads, 2, rows), f32),
        vmem((heads // 2, rows, 2 * HD), bf16), vmem((3, heads // 2, rows, 2 * HD), bf16), vmem((rows, chans), f32),
        dma((7,)), dma((3, heads)), dma((2, QUERY_HOPS, heads)), dma((2, KEY_HOPS, heads)), dma((2, KEY_HOPS, heads)),
        dma((2, QUERY_HOPS)), dma((2, KEY_HOPS)), dma((2, heads)), dma((2, QUERY_HOPS, heads)), dma((2, QUERY_HOPS, heads)),
        dma((2, 3, heads)),
    ]
    return pl.pallas_call(
        functools.partial(kernel, heads, plan(heads, chans // 128)),
        out_shape=(jax.ShapeDtypeStruct((rows, chans), bf16), jax.ShapeDtypeStruct((rows, chans), bf16)),
        in_specs=[pl.BlockSpec(memory_space=pl.ANY)] * 10,
        out_specs=[pl.BlockSpec(memory_space=pltpu.VMEM)] * 2,
        scratch_shapes=scratch,
        name="mixers",
        compiler_params=pltpu.CompilerParams(collective_id=0, has_side_effects=True, vmem_limit_bytes=60 << 20),
    )(
        hyena_q, hyena_k, hyena_v, filters, direct.reshape(1, chans), queries, keys, values,
        segment_ids.reshape(1, rows), out_weight,
    )


def solution(mesh):
    placed = (
        P("ctx", "tp"), P("ctx", "tp"), P("ctx", "tp"), P("tp", None), P("tp"),
        P("ctx", "tp"), P("ctx", "tp"), P("ctx", "tp"), P("ctx"), P(None, "tp"),
    )
    return jax.shard_map(
        local,
        mesh=mesh,
        in_specs=placed,
        out_specs=(P("ctx", "tp"), P("ctx", "tp")),
        check_vma=False,
    )
```

```python
import functools
import math

import jax
import jax.numpy as jnp
from jax import lax
from jax.experimental import pallas as pl
from jax.experimental.pallas import tpu as pltpu
from jax.sharding import PartitionSpec as P

HD = 128
WINDOW = 8
TAPS = 128
GROUP = 16
KEY_HOPS = 2
QUERY_HOPS = WINDOW - 1 - KEY_HOPS
NEG = -1e30
MESH = pl.DeviceIdType.MESH


def plan(heads, blocks):
    chunk, lag = 1.41, 1.9
    free = {"neg": 0.0, "pos": 0.0, "tp": 0.0, "mate": 0.0}
    ready = {}
    order = []
    todo = []

    def add(name, needs, cost, link=None, size=1.0, rank=0):
        todo.append(dict(name=name, needs=needs, cost=cost, link=link, size=size, rank=rank))

    for r in range(1, QUERY_HOPS + 1):
        for h in range(heads):
            add(("q", h, r), [("q", h, r - 1)] if r > 1 else [], 0.03, "neg", 1.0, r)
    for r in range(1, KEY_HOPS + 1):
        for h in range(heads):
            add(("k", h, r), [("k", h, r - 1)] if r > 1 else [], 0.03, "pos", 1.0, r)
        for h in range(heads):
            add(("v", h, r), [("v", h, r - 1)] if r > 1 else [("vt", h)], 0.03, "pos", 1.0, r)
    for h in range(heads):
        add(("vt", h), [], 0.15, rank=1)
        add(("halo", h), [("mix",), ("sent", "v", heads - 1, KEY_HOPS)], 0.03, "pos", 1.0, 5)
    add(("mix",), [], 1.0, rank=2)
    for d in range(KEY_HOPS + 1):
        add(("segk", d), [("q", 0, 1)] if d == 0 else [("k", 0, d)], 0.1, rank=3)
    for h in range(heads):
        for a in range(QUERY_HOPS, 0, -1):
            add(("part", h, a), [("q", h, a), ("k", h, KEY_HOPS), ("v", h, KEY_HOPS), ("segk", KEY_HOPS)], 0.4, rank=10 + (0 if a == QUERY_HOPS else 1))
        for d in range(KEY_HOPS + 1):
            need = [("k", h, d), ("v", h, d)] if d else [("vt", h)]
            add(("local", h, d), need + [("segk", d)] + ([("local", h, d - 1)] if d else []), 0.4, rank=20 + d)
        for a in range(QUERY_HOPS, 0, -1):
            need = [("part", h, a)] + ([("o", h, a + 1)] if a < QUERY_HOPS else [])
            add(("o", h, a), need, 0.2 if a < QUERY_HOPS else 0.05, "pos", 1.0, 4)
        add(("home", h), [("o", h, 1), ("local", h, KEY_HOPS)], 0.3, rank=5)
        add(("g0", h), [("home", h)], 0.03, "mate", 0.1, 6)
        add(("g1", h), [("home", h)], 0.03, "tp", 1.0, 5)
        add(("g2", h), [("g1", h)], 0.03, "mate", 0.1, 5)
    for p in range(heads // 2):
        for j, kind in enumerate(("home", "g0", "g1", "g2")):
            add(("proj", p, j), [(kind, 2 * p), (kind, 2 * p + 1)], 0.4, rank=30 + p * 4 + j)
    add(("taps",), [], 0.5, rank=40)
    for c in range(blocks):
        add(("hyena", c), [("taps",), ("mix",)] + [("halo", h) for h in range(heads)], 1.2, rank=50)

    now = 0.0
    while todo:
        best = None
        horizon = None
        for item in todo:
            when = 0.0
            for need in item["needs"]:
                when = max(when, ready.get(need, math.inf))
            if when <= now:
                if best is None or item["rank"] < best["rank"]:
                    best = item
            elif when < math.inf:
                horizon = when if horizon is None else min(horizon, when)
        if best is None:
            now = horizon
            continue
        todo.remove(best)
        order.append(best["name"])
        now += best["cost"]
        if best["link"]:
            begin = max(now, free[best["link"]])
            free[best["link"]] = begin + best["size"] * chunk
            ready[best["name"]] = free[best["link"]] + lag
            ready[("sent",) + best["name"]] = now
        else:
            ready[best["name"]] = now
    return order


def merge(first, second):
    high_a, total_a, sum_a = first
    high_b, total_b, sum_b = second
    high = jnp.maximum(high_a, high_b)
    fade_a, fade_b = jnp.exp2(high_a - high), jnp.exp2(high_b - high)
    return high, total_a * fade_a + total_b * fade_b, sum_a * fade_a + sum_b * fade_b


def kernel(
    heads,
    order,
    hq_hbm, hk_hbm, hv_hbm, filters_hbm, direct_hbm, q_hbm, k_hbm, v_hbm, seg_hbm, w_hbm,
    hyena_out, attn_out,
    hq, hk, hv, filters, direct, q_own, k_own, v_own, vt_own, seg_own, weight,
    q_in, segq_in, k_in, vt_in, segk_in, segk_col, ext, taps,
    part_sum, part_stat, out_sum, out_stat, in_sum, in_stat, local_sum, local_stat,
    attn, attn_in, total,
    load_sem, head_sem, q_sem, k_sem, v_sem, segq_sem, segk_sem, halo_sem, o_sem, ostat_sem, g_sem,
):
    ctx, tp = lax.axis_index("ctx"), lax.axis_index("tp")
    count = lax.axis_size("ctx")
    right, left = lax.rem(ctx + 1, count), lax.rem(ctx + count - 1, count)
    mate = tp + 1 - 2 * lax.rem(tp, 2)
    across = lax.rem(tp + 2, 4)
    diagonal = lax.rem(mate + 2, 4)
    rows, chans = hk.shape
    scale = math.log2(math.e) / math.sqrt(HD)

    loads = {}

    def load(name, source, target, sem):
        loads[name] = pltpu.make_async_copy(source, target, sem)
        loads[name].start()

    for h in range(heads):
        load(("q", h), q_hbm.at[:, pl.ds(h * HD, HD)], q_own.at[h], head_sem.at[0, h])
        load(("k", h), k_hbm.at[:, pl.ds(h * HD, HD)], k_own.at[h], head_sem.at[1, h])
        load(("v", h), v_hbm.at[:, pl.ds(h * HD, HD)], v_own.at[h], head_sem.at[2, h])
    load("seg", seg_hbm, seg_own, load_sem.at[0])
    load("hk", hk_hbm, hk, load_sem.at[1])
    load("hv", hv_hbm, hv, load_sem.at[2])
    load("filters", filters_hbm, filters, load_sem.at[3])
    load("direct", direct_hbm, direct, load_sem.at[4])
    load("hq", hq_hbm, hq, load_sem.at[5])
    load("weight", w_hbm, weight, load_sem.at[6])

    done = set()

    def loaded(name):
        if name not in done:
            done.add(name)
            loads[name].wait()

    barrier = pltpu.get_barrier_semaphore()
    for peer in ({"ctx": left}, {"ctx": right}, {"tp": mate}, {"tp": across}):
        pl.semaphore_signal(barrier, inc=1, device_id=peer, device_id_type=MESH)
    pl.semaphore_wait(barrier, 4)

    copies = {}

    def copy(name, source, target, sems, index, peer):
        copies[name] = pltpu.make_async_remote_copy(
            src_ref=source,
            dst_ref=target,
            send_sem=sems.at[(0,) + index],
            recv_sem=sems.at[(1,) + index],
            device_id=peer,
            device_id_type=MESH,
        )

    for r in range(1, QUERY_HOPS + 1):
        for h in range(heads):
            copy(("q", h, r), q_own.at[h] if r == 1 else q_in.at[r - 2, h], q_in.at[r - 1, h], q_sem, (r - 1, h), {"ctx": left})
            copy(("o", h, r), out_sum.at[r - 1, h], in_sum.at[r - 1, h], o_sem, (r - 1, h), {"ctx": right})
            copy(("ostat", h, r), out_stat.at[r - 1, h], in_stat.at[r - 1, h], ostat_sem, (r - 1, h), {"ctx": right})
        copy(("segq", r), seg_own if r == 1 else segq_in.at[r - 2], segq_in.at[r - 1], segq_sem, (r - 1,), {"ctx": left})
    for r in range(1, KEY_HOPS + 1):
        for h in range(heads):
            copy(("k", h, r), k_own.at[h] if r == 1 else k_in.at[r - 2, h], k_in.at[r - 1, h], k_sem, (r - 1, h), {"ctx": right})
            copy(("v", h, r), vt_own.at[h] if r == 1 else vt_in.at[r - 2, h], vt_in.at[r - 1, h], v_sem, (r - 1, h), {"ctx": right})
        copy(("segk", r), seg_own if r == 1 else segk_in.at[r - 2], segk_in.at[r - 1], segk_sem, (r - 1,), {"ctx": right})
    strip = chans // heads
    for h in range(heads):
        lanes = pl.ds(h * strip, strip)
        copy(("halo", h), ext.at[pl.ds(rows, TAPS), lanes], ext.at[pl.ds(0, TAPS), lanes], halo_sem, (h,), {"ctx": right})
        half = pl.ds(h % 2 * HD, HD)
        mine = attn.at[h // 2, :, half]
        copy(("g0", h), mine, attn_in.at[0, h // 2, :, half], g_sem, (0, h), {"tp": mate})
        copy(("g1", h), mine, attn_in.at[1, h // 2, :, half], g_sem, (1, h), {"tp": across})
        copy(("g2", h), attn_in.at[1, h // 2, :, half], attn_in.at[2, h // 2, :, half], g_sem, (2, h), {"tp": mate})

    got = set()

    def arrived(name):
        if name not in got:
            got.add(name)
            copies[name].wait_recv()

    def send(name):
        copies[name].start()

    def column(row):
        return jnp.transpose(jnp.broadcast_to(row.astype(jnp.float32), (HD, rows)))

    def partial(query, query_seg, key, value_t, key_col, causal):
        score = lax.dot_general(key[...], query[...], (((1,), (1,)), ((), ())), preferred_element_type=jnp.float32)
        col = key_col[...]
        allowed = jnp.concatenate([col] * (rows // HD), axis=1) == query_seg[...].astype(jnp.float32)
        if causal:
            allowed = allowed & (
                lax.broadcasted_iota(jnp.int32, (rows, rows), 0) <= lax.broadcasted_iota(jnp.int32, (rows, rows), 1)
            )
        score = jnp.where(allowed, score * scale, NEG)
        high = jnp.max(score, axis=0, keepdims=True)
        expo = jnp.exp2(score - high)
        amount = jnp.sum(expo, axis=0, keepdims=True)
        summed = jnp.dot(value_t[...], expo.astype(jnp.bfloat16), preferred_element_type=jnp.float32)
        return high, amount, summed

    def keep(state, stat_ref, sum_ref):
        stat_ref[0:1, :] = state[0]
        stat_ref[1:2, :] = state[1]
        sum_ref[...] = state[2].astype(sum_ref.dtype)

    def fetch(stat_ref, sum_ref):
        return stat_ref[0:1, :], stat_ref[1:2, :], sum_ref[...].astype(jnp.float32)

    def step_q(h, r):
        if r == 1:
            loaded(("q", h))
            if h == 0:
                loaded("seg")
        else:
            arrived(("q", h, r - 1))
            if h == 0:
                arrived(("segq", r - 1))
        if h == 0:
            send(("segq", r))
        send(("q", h, r))

    def step_k(h, r):
        if r == 1:
            loaded(("k", h))
            if h == 0:
                loaded("seg")
        else:
            arrived(("k", h, r - 1))
            if h == 0:
                arrived(("segk", r - 1))
        if h == 0:
            send(("segk", r))
        send(("k", h, r))

    def step_vt(h):
        loaded(("v", h))
        vt_own[h] = jnp.transpose(v_own[h])

    def step_v(h, r):
        if r > 1:
            arrived(("v", h, r - 1))
        send(("v", h, r))

    def step_mix():
        loaded("hk")
        loaded("hv")
        for lo in range(0, rows, 64):
            ext[pl.ds(TAPS + lo, 64), :] = (
                hk[pl.ds(lo, 64), :].astype(jnp.float32) * hv[pl.ds(lo, 64), :].astype(jnp.float32)
            ).astype(jnp.bfloat16)

    def step_halo(h):
        send(("halo", h))

    def step_segk(d):
        if d == 0:
            loaded("seg")
            segk_col[0] = column(seg_own[...])
        else:
            arrived(("segk", d))
            segk_col[d] = column(segk_in[d - 1])

    def step_part(h, a):
        arrived(("q", h, a))
        arrived(("segq", a))
        arrived(("k", h, KEY_HOPS))
        arrived(("v", h, KEY_HOPS))
        state = partial(q_in.at[a - 1, h], segq_in.at[a - 1], k_in.at[KEY_HOPS - 1, h], vt_in.at[KEY_HOPS - 1, h], segk_col.at[KEY_HOPS], False)
        if a == QUERY_HOPS:
            keep(state, out_stat.at[a - 1, h], out_sum.at[a - 1, h])
        else:
            keep(state, part_stat.at[a - 1, h], part_sum.at[a - 1, h])

    def step_local(h, d):
        if d == 0:
            state = partial(q_own.at[h], seg_own, k_own.at[h], vt_own.at[h], segk_col.at[0], True)
        else:
            arrived(("k", h, d))
            arrived(("v", h, d))
            state = partial(q_own.at[h], seg_own, k_in.at[d - 1, h], vt_in.at[d - 1, h], segk_col.at[d], False)
            state = merge(fetch(local_stat.at[h], local_sum.at[h]), state)
        keep(state, local_stat.at[h], local_sum.at[h])

    def step_o(h, a):
        if a < QUERY_HOPS:
            arrived(("o", h, a + 1))
            arrived(("ostat", h, a + 1))
            state = merge(fetch(part_stat.at[a - 1, h], part_sum.at[a - 1, h]), fetch(in_stat.at[a, h], in_sum.at[a, h]))
            keep(state, out_stat.at[a - 1, h], out_sum.at[a - 1, h])
        send(("o", h, a))
        send(("ostat", h, a))

    def step_home(h):
        arrived(("o", h, 1))
        arrived(("ostat", h, 1))
        _, amount, summed = merge(fetch(local_stat.at[h], local_sum.at[h]), fetch(in_stat.at[0, h], in_sum.at[0, h]))
        result = jnp.transpose(summed / amount)
        attn[h // 2, :, pl.ds(h % 2 * HD, HD)] = result.astype(jnp.bfloat16)

    def step_g0(h):
        send(("g0", h))

    def step_g1(h):
        send(("g1", h))

    def step_g2(h):
        arrived(("g1", h))
        send(("g2", h))

    projected = []
    width = 256

    def step_proj(p, j):
        loaded("weight")
        if j:
            for h in (2 * p, 2 * p + 1):
                arrived((("g0", "g1", "g2")[j - 1], h))
        block = attn[p] if j == 0 else attn_in[j - 1, p]
        owner = (tp, mate, across, diagonal)[j]
        start = pl.multiple_of(owner * (heads * HD) + p * 2 * HD, 2 * HD)
        first, last = not projected, len(projected) == 2 * heads - 1
        projected.append((p, j))
        for lo in range(0, chans, width):
            lanes = pl.ds(lo, width)
            term = jnp.dot(block, weight[pl.ds(start, 2 * HD), lanes], preferred_element_type=jnp.float32)
            if not first:
                term = total[:, lanes] + term
            if last:
                attn_out[:, lanes] = term.astype(jnp.bfloat16)
            else:
                total[:, lanes] = term

    def step_taps():
        loaded("filters")
        tap = lax.broadcasted_iota(jnp.int32, (TAPS, 2 * TAPS), 0)
        place = lax.broadcasted_iota(jnp.int32, (TAPS, 2 * TAPS), 1)
        flip = jnp.where(tap + place == TAPS, 1.0, 0.0).astype(jnp.bfloat16)
        taps[...] = jnp.dot(filters[...], flip, preferred_element_type=jnp.float32)

    def step_hyena(c):
        if c == 0:
            for h in range(heads):
                arrived(("halo", h))
            loaded("hq")
            loaded("direct")
        lanes = pl.ds(c * 128, 128)
        before = ext[pl.ds(0, TAPS), lanes]
        before = jnp.where(ctx == 0, jnp.zeros_like(before), before)
        upper, lower = ext[pl.ds(TAPS, TAPS), lanes], ext[pl.ds(2 * TAPS, TAPS), lanes]
        data = jnp.concatenate(
            [jnp.concatenate([before, upper], axis=0), jnp.concatenate([upper, lower], axis=0)], axis=1
        )
        group = lax.rem(lax.broadcasted_iota(jnp.int32, (TAPS, 2 * TAPS), 1), 128) // GROUP
        conv = jnp.zeros((TAPS, 2 * TAPS), jnp.float32)
        per = 128 // GROUP
        for g in range(per):
            row = jnp.broadcast_to(taps[pl.ds(c * per + g, 1), :], (TAPS, 2 * TAPS))
            table = pltpu.roll(row, 0, 1, stride=1, stride_axis=0).astype(jnp.bfloat16)
            conv = jnp.where(group == g, jnp.dot(table, data, preferred_element_type=jnp.float32), conv)
        gain = direct[...].astype(jnp.float32)[c : c + 1, :]
        for b, mixed in enumerate((upper, lower)):
            span = pl.ds(b * TAPS, TAPS)
            hyena_out[span, lanes] = (
                hq[span, lanes].astype(jnp.float32)
                * (conv[:, b * TAPS : (b + 1) * TAPS] + gain * mixed.astype(jnp.float32))
            ).astype(jnp.bfloat16)

    steps = dict(
        q=step_q, k=step_k, vt=step_vt, v=step_v, mix=step_mix, halo=step_halo, segk=step_segk, part=step_part,
        local=step_local, o=step_o, home=step_home, g0=step_g0, g1=step_g1, g2=step_g2, proj=step_proj,
        taps=step_taps, hyena=step_hyena,
    )
    for name in order:
        steps[name[0]](*name[1:])
    for name in copies:
        arrived(name)
        copies[name].wait_send()


def deliver(hyena_ref, attn_ref, hyena_out, attn_out, hyena_buf, attn_buf, sems):
    size = hyena_buf.shape[1]
    loads, stores = [], []
    for i, (source, target, buf) in enumerate(((hyena_ref, hyena_out, hyena_buf), (attn_ref, attn_out, attn_buf))):
        for j in range(2):
            span = pl.ds(j * size, size)
            loads.append(pltpu.make_async_copy(source.at[span, :], buf.at[j], sems.at[0, 2 * i + j]))
            stores.append(pltpu.make_async_copy(buf.at[j], target.at[span, :], sems.at[1, 2 * i + j]))
    for move in loads:
        move.start()
    for move, store in zip(loads, stores):
        move.wait()
        store.start()
    for store in stores:
        store.wait()


def local(hyena_q, hyena_k, hyena_v, filters, direct, queries, keys, values, segment_ids, out_weight):
    rows, feat = queries.shape
    chans = hyena_k.shape[1]
    heads = feat // HD
    groups = filters.shape[0]
    depth = out_weight.shape[0]
    bf16, f32, i32 = jnp.bfloat16, jnp.float32, jnp.int32
    dma = pltpu.SemaphoreType.DMA
    vmem = pltpu.VMEM
    scratch = [
        vmem((rows, chans), bf16), vmem((rows, chans), bf16), vmem((rows, chans), bf16),
        vmem((groups, TAPS), bf16), vmem((chans // HD, HD), bf16),
        vmem((heads, rows, HD), bf16), vmem((heads, rows, HD), bf16), vmem((heads, rows, HD), bf16),
        vmem((heads, HD, rows), bf16), vmem((1, rows), i32), vmem((depth, chans), bf16),
        vmem((QUERY_HOPS, heads, rows, HD), bf16), vmem((QUERY_HOPS, 1, rows), i32),
        vmem((KEY_HOPS, heads, rows, HD), bf16), vmem((KEY_HOPS, heads, HD, rows), bf16), vmem((KEY_HOPS, 1, rows), i32),
        vmem((KEY_HOPS + 1, rows, HD), f32), vmem((TAPS + rows, chans), bf16), vmem((groups, 2 * TAPS), f32),
        vmem((QUERY_HOPS, heads, HD, rows), f32), vmem((QUERY_HOPS, heads, 2, rows), f32),
        vmem((QUERY_HOPS, heads, HD, rows), bf16), vmem((QUERY_HOPS, heads, 2, rows), f32),
        vmem((QUERY_HOPS, heads, HD, rows), bf16), vmem((QUERY_HOPS, heads, 2, rows), f32),
        vmem((heads, HD, rows), f32), vmem((heads, 2, rows), f32),
        vmem((heads // 2, rows, 2 * HD), bf16), vmem((3, heads // 2, rows, 2 * HD), bf16), vmem((rows, chans), f32),
        dma((7,)), dma((3, heads)), dma((2, QUERY_HOPS, heads)), dma((2, KEY_HOPS, heads)), dma((2, KEY_HOPS, heads)),
        dma((2, QUERY_HOPS)), dma((2, KEY_HOPS)), dma((2, heads)), dma((2, QUERY_HOPS, heads)), dma((2, QUERY_HOPS, heads)),
        dma((2, 3, heads)),
    ]
    hyena_out, attn_out = pl.pallas_call(
        functools.partial(kernel, heads, plan(heads, chans // 128)),
        out_shape=(jax.ShapeDtypeStruct((rows, chans), bf16), jax.ShapeDtypeStruct((rows, chans), bf16)),
        in_specs=[pl.BlockSpec(memory_space=pl.ANY)] * 10,
        out_specs=[pl.BlockSpec(memory_space=pltpu.VMEM)] * 2,
        scratch_shapes=scratch,
        name="mixers",
        compiler_params=pltpu.CompilerParams(collective_id=0, has_side_effects=True, vmem_limit_bytes=60 << 20),
    )(
        hyena_q, hyena_k, hyena_v, filters, direct.reshape(chans // HD, HD), queries, keys, values,
        segment_ids.reshape(1, rows), out_weight,
    )
    half = vmem((2, rows // 2, chans), bf16)
    return pl.pallas_call(
        deliver,
        out_shape=(jax.ShapeDtypeStruct((rows, chans), bf16), jax.ShapeDtypeStruct((rows, chans), bf16)),
        in_specs=[pl.BlockSpec(memory_space=pl.ANY)] * 2,
        out_specs=[pl.BlockSpec(memory_space=pl.ANY)] * 2,
        scratch_shapes=[half, half, dma((2, 4))],
        name="deliver",
        compiler_params=pltpu.CompilerParams(vmem_limit_bytes=60 << 20),
    )(hyena_out, attn_out)


def solution(mesh):
    placed = (
        P("ctx", "tp"), P("ctx", "tp"), P("ctx", "tp"), P("tp", None), P("tp"),
        P("ctx", "tp"), P("ctx", "tp"), P("ctx", "tp"), P("ctx"), P(None, "tp"),
    )
    return jax.shard_map(
        local,
        mesh=mesh,
        in_specs=placed,
        out_specs=(P("ctx", "tp"), P("ctx", "tp")),
        check_vma=False,
    )
```

```python
import functools
import math

import jax
import jax.numpy as jnp
from jax import lax
from jax.experimental import pallas as pl
from jax.experimental.pallas import tpu as pltpu
from jax.sharding import PartitionSpec as P

HD = 128
WINDOW = 8
TAPS = 128
GROUP = 16
KEY_HOPS = 2
QUERY_HOPS = WINDOW - 1 - KEY_HOPS
NEG = -1e30
PARTS = 2
WEIGHTS = dict(qh=0.5, qr=-2.515, kh=0.614, kr=-2.285, k0=1.574, v0=-0.472, halo=14.128, o0=13.001, oh=5, oa=-0.97, ph=-3.06, pa=1, loc=150.0, mix=-11.49, hy=500.0, lq=1.187, lp=0.13, thr=99)
MESH = pl.DeviceIdType.MESH


def plan(heads, blocks):
    chunk, lag = 1.41, 1.9
    w = WEIGHTS
    size = 1.0 / PARTS
    steps = {}

    def add(name, needs, cost, link=None, amount=1.0, rank=0.0):
        steps[name] = (needs, cost, link, amount, rank)

    for h in range(heads):
        for r in range(1, KEY_HOPS + 1):
            turn = w["kh"] * h + w["kr"] * r
            add(("k", h, r), [("k", h, r - 1)] if r > 1 else [], 0.03, "pos", 1.0, turn + w["k0"])
            add(("v", h, r), [("v", h, r - 1)] if r > 1 else [("vt", h)], 0.03, "pos", 1.0, turn + w["v0"])
        add(("vt", h), [], 0.15, rank=h - 100)
        add(("halo", h), [("mix",)], 0.03, "pos", 1.0, w["halo"])
        for v in range(h * PARTS, (h + 1) * PARTS):
            at = v / PARTS
            for r in range(1, QUERY_HOPS + 1):
                add(("q", v, r), [("q", v, r - 1)] if r > 1 else [], 0.03, "neg", size, w["qh"] * at + w["qr"] * r)
            for a in range(QUERY_HOPS, 0, -1):
                needs = [("q", v, a), ("q", 0, a), ("vt", h), ("k", h, KEY_HOPS), ("v", h, KEY_HOPS), ("segk", KEY_HOPS)]
                add(("part", v, a), needs, 0.05 + 0.35 * size, rank=100 + w["ph"] * at - w["pa"] * a)
                needs = [("part", v, a)] + ([("o", v, a + 1)] if a < QUERY_HOPS else [])
                cost = 0.07 + 0.13 * size if a < QUERY_HOPS else 0.05
                add(("o", v, a), needs, cost, "pos", size, w["o0"] + w["oh"] * at - w["oa"] * a)
            for d in range(KEY_HOPS + 1):
                needs = [("k", h, d), ("v", h, d)] if d else [("vt", h)]
                needs = needs + [("segk", d)] + ([("local", v, d - 1)] if d else [])
                add(("local", v, d), needs, 0.05 + 0.35 * size, rank=w["loc"] + at)
            add(("home", v), [("o", v, 1), ("local", v, KEY_HOPS)], 0.1 + 0.2 * size, rank=-50)
            add(("g0", v), [("home", v)], 0.03, "mate", 0.1 * size, -40)
            add(("g1", v), [("home", v)], 0.03, "tp", size, -45)
            add(("g2", v), [("g1", v)], 0.03, "mate", 0.1 * size, -45)
    for d in range(KEY_HOPS + 1):
        add(("segk", d), [("k", 0, d)] if d else [], 0.1, rank=90)
    add(("mix",), [], 1.0, rank=w["mix"])
    for p in range(heads // 2):
        for j, kind in enumerate(("home", "g0", "g1", "g2")):
            needs = [(kind, v) for v in range(2 * p * PARTS, 2 * (p + 1) * PARTS)]
            add(("proj", p, j), needs, 0.4, rank=300 + 4 * p + j)
    add(("taps",), [], 0.5, rank=400)
    for c in range(blocks):
        add(("hyena", c), [("taps",), ("mix",)] + [("halo", h) for h in range(heads)], 1.2, rank=w["hy"])

    users = {name: [] for name in steps}
    missing, when = {}, {}
    for name, (needs, *_) in steps.items():
        missing[name], when[name] = len(needs), 0.0
        for need in needs:
            users[need].append(name)
    free = dict(neg=0.0, pos=0.0, tp=0.0, mate=0.0)
    lags = dict(neg=lag + w["lq"], pos=lag + w["lp"], tp=lag, mate=0.95)
    waiting = [name for name in steps if not missing[name]]
    order, now = [], 0.0
    while waiting:
        best, best_key, later = None, None, math.inf
        for name in waiting:
            _, _, link, _, rank = steps[name]
            begin = max(when[name], free[link] - w["thr"]) if link else when[name]
            if begin <= now + 1e-9:
                key = (0 if link or name[0] in ("vt", "home") else 1, rank)
                if best is None or key < best_key:
                    best, best_key = name, key
            else:
                later = min(later, begin)
        if best is None:
            now = later
            continue
        waiting.remove(best)
        order.append(best)
        _, cost, link, amount, _ = steps[best]
        now += cost
        done = now
        if link:
            free[link] = max(now, free[link]) + amount * chunk
            done = free[link] + lags[link]
        for user in users[best]:
            missing[user] -= 1
            when[user] = max(when[user], done)
            if not missing[user]:
                waiting.append(user)
    return order


def merge(first, second):
    high_a, total_a, sum_a = first
    high_b, total_b, sum_b = second
    high = jnp.maximum(high_a, high_b)
    fade_a, fade_b = jnp.exp2(high_a - high), jnp.exp2(high_b - high)
    return high, total_a * fade_a + total_b * fade_b, sum_a * fade_a + sum_b * fade_b


def kernel(
    heads,
    order,
    hq_hbm, hk_hbm, hv_hbm, filters_hbm, direct_hbm, q_hbm, k_hbm, v_hbm, seg_hbm, w_hbm,
    hyena_out, attn_out,
    hq, hk, hv, filters, direct, q_own, k_own, v_own, vt_own, seg_own, weight,
    q_in, segq_in, k_in, vt_in, segk_in, segk_col, ext, taps,
    part_sum, part_stat, out_sum, out_stat, in_sum, in_stat, local_sum, local_stat,
    attn, attn_in, total,
    load_sem, head_sem, q_sem, k_sem, v_sem, segq_sem, segk_sem, halo_sem, o_sem, ostat_sem, g_sem,
):
    ctx, tp = lax.axis_index("ctx"), lax.axis_index("tp")
    count = lax.axis_size("ctx")
    right, left = lax.rem(ctx + 1, count), lax.rem(ctx + count - 1, count)
    mate = tp + 1 - 2 * lax.rem(tp, 2)
    across = lax.rem(tp + 2, 4)
    diagonal = lax.rem(mate + 2, 4)
    rows, chans = hk.shape
    scale = math.log2(math.e) / math.sqrt(HD)
    piece = rows // PARTS

    def span_of(v):
        return pl.ds(v % PARTS * piece, piece)

    loads = {}

    def load(name, source, target, sem):
        loads[name] = pltpu.make_async_copy(source, target, sem)
        loads[name].start()

    for h in range(heads):
        load(("q", h), q_hbm.at[:, pl.ds(h * HD, HD)], q_own.at[h], head_sem.at[0, h])
        load(("k", h), k_hbm.at[:, pl.ds(h * HD, HD)], k_own.at[h], head_sem.at[1, h])
        load(("v", h), v_hbm.at[:, pl.ds(h * HD, HD)], v_own.at[h], head_sem.at[2, h])
    load("seg", seg_hbm, seg_own, load_sem.at[0])
    load("hk", hk_hbm, hk, load_sem.at[1])
    load("hv", hv_hbm, hv, load_sem.at[2])
    load("filters", filters_hbm, filters, load_sem.at[3])
    load("direct", direct_hbm, direct, load_sem.at[4])
    load("hq", hq_hbm, hq, load_sem.at[5])
    load("weight", w_hbm, weight, load_sem.at[6])

    done = set()

    def loaded(name):
        if name not in done:
            done.add(name)
            loads[name].wait()

    barrier = pltpu.get_barrier_semaphore()
    for peer in ({"ctx": left}, {"ctx": right}, {"tp": mate}, {"tp": across}):
        pl.semaphore_signal(barrier, inc=1, device_id=peer, device_id_type=MESH)
    pl.semaphore_wait(barrier, 4)

    copies = {}

    def copy(name, source, target, sems, index, peer):
        copies[name] = pltpu.make_async_remote_copy(
            src_ref=source,
            dst_ref=target,
            send_sem=sems.at[(0,) + index],
            recv_sem=sems.at[(1,) + index],
            device_id=peer,
            device_id_type=MESH,
        )

    for r in range(1, QUERY_HOPS + 1):
        for v in range(heads * PARTS):
            source = q_own.at[v // PARTS] if r == 1 else q_in.at[r - 2, v // PARTS]
            target = q_in.at[r - 1, v // PARTS]
            copy(("q", v, r), source.at[span_of(v), :], target.at[span_of(v), :], q_sem, (r - 1, v), {"ctx": left})
            copy(("o", v, r), out_sum.at[r - 1, v], in_sum.at[r - 1, v], o_sem, (r - 1, v), {"ctx": right})
            copy(("ostat", v, r), out_stat.at[r - 1, v], in_stat.at[r - 1, v], ostat_sem, (r - 1, v), {"ctx": right})
        copy(("segq", r), seg_own if r == 1 else segq_in.at[r - 2], segq_in.at[r - 1], segq_sem, (r - 1,), {"ctx": left})
    for r in range(1, KEY_HOPS + 1):
        for h in range(heads):
            copy(("k", h, r), k_own.at[h] if r == 1 else k_in.at[r - 2, h], k_in.at[r - 1, h], k_sem, (r - 1, h), {"ctx": right})
            copy(("v", h, r), vt_own.at[h] if r == 1 else vt_in.at[r - 2, h], vt_in.at[r - 1, h], v_sem, (r - 1, h), {"ctx": right})
        copy(("segk", r), seg_own if r == 1 else segk_in.at[r - 2], segk_in.at[r - 1], segk_sem, (r - 1,), {"ctx": right})
    strip = chans // heads
    for h in range(heads):
        lanes = pl.ds(h * strip, strip)
        copy(("halo", h), ext.at[pl.ds(rows, TAPS), lanes], ext.at[pl.ds(0, TAPS), lanes], halo_sem, (h,), {"ctx": right})
    for v in range(heads * PARTS):
        h = v // PARTS
        spot = (h // 2, span_of(v), pl.ds(h % 2 * HD, HD))
        copy(("g0", v), attn.at[spot], attn_in.at[(0,) + spot], g_sem, (0, v), {"tp": mate})
        copy(("g1", v), attn.at[spot], attn_in.at[(1,) + spot], g_sem, (1, v), {"tp": across})
        copy(("g2", v), attn_in.at[(1,) + spot], attn_in.at[(2,) + spot], g_sem, (2, v), {"tp": mate})

    got = set()

    def arrived(name):
        if name not in got:
            got.add(name)
            copies[name].wait_recv()

    def send(name):
        copies[name].start()

    def column(row):
        return jnp.transpose(jnp.broadcast_to(row.astype(jnp.float32), (HD, rows)))

    def partial(query, query_seg, v, key, value_t, key_col, causal):
        score = lax.dot_general(
            key[...], query[span_of(v), :], (((1,), (1,)), ((), ())), preferred_element_type=jnp.float32
        )
        col = key_col[:, :piece] if piece <= HD else jnp.concatenate([key_col[...]] * (piece // HD), axis=1)
        allowed = col == query_seg[:, span_of(v)].astype(jnp.float32)
        if causal:
            allowed = allowed & (
                lax.broadcasted_iota(jnp.int32, (rows, piece), 0)
                <= lax.broadcasted_iota(jnp.int32, (rows, piece), 1) + v % PARTS * piece
            )
        score = jnp.where(allowed, score * scale, NEG)
        high = jnp.max(score, axis=0, keepdims=True)
        expo = jnp.exp2(score - high)
        amount = jnp.sum(expo, axis=0, keepdims=True)
        summed = jnp.dot(value_t[...], expo.astype(jnp.bfloat16), preferred_element_type=jnp.float32)
        return high, amount, summed

    def keep(state, stat_ref, sum_ref):
        stat_ref[0:1, :] = state[0]
        stat_ref[1:2, :] = state[1]
        sum_ref[...] = state[2].astype(sum_ref.dtype)

    def fetch(stat_ref, sum_ref):
        return stat_ref[0:1, :], stat_ref[1:2, :], sum_ref[...].astype(jnp.float32)

    def step_q(v, r):
        if r == 1:
            loaded(("q", v // PARTS))
            if v == 0:
                loaded("seg")
        else:
            arrived(("q", v, r - 1))
            if v == 0:
                arrived(("segq", r - 1))
        if v == 0:
            send(("segq", r))
        send(("q", v, r))

    def step_k(h, r):
        if r == 1:
            loaded(("k", h))
            if h == 0:
                loaded("seg")
        else:
            arrived(("k", h, r - 1))
            if h == 0:
                arrived(("segk", r - 1))
        if h == 0:
            send(("segk", r))
        send(("k", h, r))

    def step_vt(h):
        loaded(("v", h))
        vt_own[h] = jnp.transpose(v_own[h])

    def step_v(h, r):
        if r > 1:
            arrived(("v", h, r - 1))
        send(("v", h, r))

    def step_mix():
        loaded("hk")
        loaded("hv")
        for lo in range(0, rows, 64):
            ext[pl.ds(TAPS + lo, 64), :] = (
                hk[pl.ds(lo, 64), :].astype(jnp.float32) * hv[pl.ds(lo, 64), :].astype(jnp.float32)
            ).astype(jnp.bfloat16)

    def step_halo(h):
        send(("halo", h))

    def step_segk(d):
        if d == 0:
            loaded("seg")
            segk_col[0] = column(seg_own[...])
        else:
            arrived(("segk", d))
            segk_col[d] = column(segk_in[d - 1])

    def step_part(v, a):
        h = v // PARTS
        arrived(("q", v, a))
        arrived(("segq", a))
        arrived(("k", h, KEY_HOPS))
        arrived(("v", h, KEY_HOPS))
        last = KEY_HOPS - 1
        state = partial(q_in.at[a - 1, h], segq_in.at[a - 1], v, k_in.at[last, h], vt_in.at[last, h], segk_col.at[KEY_HOPS], False)
        if a == QUERY_HOPS:
            keep(state, out_stat.at[a - 1, v], out_sum.at[a - 1, v])
        else:
            keep(state, part_stat.at[a - 1, v], part_sum.at[a - 1, v])

    def step_local(v, d):
        h = v // PARTS
        if d == 0:
            state = partial(q_own.at[h], seg_own, v, k_own.at[h], vt_own.at[h], segk_col.at[0], True)
        else:
            arrived(("k", h, d))
            arrived(("v", h, d))
            state = partial(q_own.at[h], seg_own, v, k_in.at[d - 1, h], vt_in.at[d - 1, h], segk_col.at[d], False)
            state = merge(fetch(local_stat.at[v], local_sum.at[v]), state)
        keep(state, local_stat.at[v], local_sum.at[v])

    def step_o(v, a):
        if a < QUERY_HOPS:
            arrived(("ostat", v, a + 1))
            arrived(("o", v, a + 1))
            state = merge(fetch(part_stat.at[a - 1, v], part_sum.at[a - 1, v]), fetch(in_stat.at[a, v], in_sum.at[a, v]))
            keep(state, out_stat.at[a - 1, v], out_sum.at[a - 1, v])
        send(("ostat", v, a))
        send(("o", v, a))

    def step_home(v):
        h = v // PARTS
        arrived(("ostat", v, 1))
        arrived(("o", v, 1))
        _, amount, summed = merge(fetch(local_stat.at[v], local_sum.at[v]), fetch(in_stat.at[0, v], in_sum.at[0, v]))
        result = jnp.transpose(summed / amount)
        attn[h // 2, span_of(v), pl.ds(h % 2 * HD, HD)] = result.astype(jnp.bfloat16)

    def step_g0(h):
        send(("g0", h))

    def step_g1(h):
        send(("g1", h))

    def step_g2(h):
        arrived(("g1", h))
        send(("g2", h))

    projected = []
    width = 256

    def step_proj(p, j):
        loaded("weight")
        if j:
            for h in range(2 * p * PARTS, 2 * (p + 1) * PARTS):
                arrived((("g0", "g1", "g2")[j - 1], h))
        block = attn[p] if j == 0 else attn_in[j - 1, p]
        owner = (tp, mate, across, diagonal)[j]
        start = pl.multiple_of(owner * (heads * HD) + p * 2 * HD, 2 * HD)
        first, last = not projected, len(projected) == 2 * heads - 1
        projected.append((p, j))
        for lo in range(0, chans, width):
            lanes = pl.ds(lo, width)
            term = jnp.dot(block, weight[pl.ds(start, 2 * HD), lanes], preferred_element_type=jnp.float32)
            if not first:
                term = total[:, lanes] + term
            if last:
                attn_out[:, lanes] = term.astype(jnp.bfloat16)
            else:
                total[:, lanes] = term

    def step_taps():
        loaded("filters")
        tap = lax.broadcasted_iota(jnp.int32, (TAPS, 2 * TAPS), 0)
        place = lax.broadcasted_iota(jnp.int32, (TAPS, 2 * TAPS), 1)
        flip = jnp.where(tap + place == TAPS, 1.0, 0.0).astype(jnp.bfloat16)
        taps[...] = jnp.dot(filters[...], flip, preferred_element_type=jnp.float32)

    def step_hyena(c):
        if c == 0:
            for h in range(heads):
                arrived(("halo", h))
            loaded("hq")
            loaded("direct")
        lanes = pl.ds(c * 128, 128)
        before = ext[pl.ds(0, TAPS), lanes]
        before = jnp.where(ctx == 0, jnp.zeros_like(before), before)
        upper, lower = ext[pl.ds(TAPS, TAPS), lanes], ext[pl.ds(2 * TAPS, TAPS), lanes]
        data = jnp.concatenate(
            [jnp.concatenate([before, upper], axis=0), jnp.concatenate([upper, lower], axis=0)], axis=1
        )
        group = lax.rem(lax.broadcasted_iota(jnp.int32, (TAPS, 2 * TAPS), 1), 128) // GROUP
        conv = jnp.zeros((TAPS, 2 * TAPS), jnp.float32)
        per = 128 // GROUP
        for g in range(per):
            row = jnp.broadcast_to(taps[pl.ds(c * per + g, 1), :], (TAPS, 2 * TAPS))
            table = pltpu.roll(row, 0, 1, stride=1, stride_axis=0).astype(jnp.bfloat16)
            conv = jnp.where(group == g, jnp.dot(table, data, preferred_element_type=jnp.float32), conv)
        gain = direct[...].astype(jnp.float32)[c : c + 1, :]
        for b, mixed in enumerate((upper, lower)):
            span = pl.ds(b * TAPS, TAPS)
            hyena_out[span, lanes] = (
                hq[span, lanes].astype(jnp.float32)
                * (conv[:, b * TAPS : (b + 1) * TAPS] + gain * mixed.astype(jnp.float32))
            ).astype(jnp.bfloat16)

    steps = dict(
        q=step_q, k=step_k, vt=step_vt, v=step_v, mix=step_mix, halo=step_halo, segk=step_segk, part=step_part,
        local=step_local, o=step_o, home=step_home, g0=step_g0, g1=step_g1, g2=step_g2, proj=step_proj,
        taps=step_taps, hyena=step_hyena,
    )
    for name in order:
        steps[name[0]](*name[1:])
    for name in copies:
        arrived(name)
        copies[name].wait_send()


def deliver(hyena_ref, attn_ref, hyena_out, attn_out, hyena_buf, attn_buf, sems):
    size = hyena_buf.shape[1]
    loads, stores = [], []
    for i, (source, target, buf) in enumerate(((hyena_ref, hyena_out, hyena_buf), (attn_ref, attn_out, attn_buf))):
        for j in range(2):
            span = pl.ds(j * size, size)
            loads.append(pltpu.make_async_copy(source.at[span, :], buf.at[j], sems.at[0, 2 * i + j]))
            stores.append(pltpu.make_async_copy(buf.at[j], target.at[span, :], sems.at[1, 2 * i + j]))
    for move in loads:
        move.start()
    for move, store in zip(loads, stores):
        move.wait()
        store.start()
    for store in stores:
        store.wait()


def local(hyena_q, hyena_k, hyena_v, filters, direct, queries, keys, values, segment_ids, out_weight):
    rows, feat = queries.shape
    chans = hyena_k.shape[1]
    heads = feat // HD
    groups = filters.shape[0]
    depth = out_weight.shape[0]
    pieces, piece = heads * PARTS, rows // PARTS
    bf16, f32, i32 = jnp.bfloat16, jnp.float32, jnp.int32
    dma = pltpu.SemaphoreType.DMA
    vmem = pltpu.VMEM
    scratch = [
        vmem((rows, chans), bf16), vmem((rows, chans), bf16), vmem((rows, chans), bf16),
        vmem((groups, TAPS), bf16), vmem((chans // HD, HD), bf16),
        vmem((heads, rows, HD), bf16), vmem((heads, rows, HD), bf16), vmem((heads, rows, HD), bf16),
        vmem((heads, HD, rows), bf16), vmem((1, rows), i32), vmem((depth, chans), bf16),
        vmem((QUERY_HOPS, heads, rows, HD), bf16), vmem((QUERY_HOPS, 1, rows), i32),
        vmem((KEY_HOPS, heads, rows, HD), bf16), vmem((KEY_HOPS, heads, HD, rows), bf16), vmem((KEY_HOPS, 1, rows), i32),
        vmem((KEY_HOPS + 1, rows, HD), f32), vmem((TAPS + rows, chans), bf16), vmem((groups, 2 * TAPS), f32),
        vmem((QUERY_HOPS, pieces, HD, piece), f32), vmem((QUERY_HOPS, pieces, 2, piece), f32),
        vmem((QUERY_HOPS, pieces, HD, piece), bf16), vmem((QUERY_HOPS, pieces, 2, piece), f32),
        vmem((QUERY_HOPS, pieces, HD, piece), bf16), vmem((QUERY_HOPS, pieces, 2, piece), f32),
        vmem((pieces, HD, piece), f32), vmem((pieces, 2, piece), f32),
        vmem((heads // 2, rows, 2 * HD), bf16), vmem((3, heads // 2, rows, 2 * HD), bf16), vmem((rows, chans), f32),
        dma((7,)), dma((3, heads)), dma((2, QUERY_HOPS, pieces)), dma((2, KEY_HOPS, heads)), dma((2, KEY_HOPS, heads)),
        dma((2, QUERY_HOPS)), dma((2, KEY_HOPS)), dma((2, heads)), dma((2, QUERY_HOPS, pieces)), dma((2, QUERY_HOPS, pieces)),
        dma((2, 3, pieces)),
    ]
    hyena_out, attn_out = pl.pallas_call(
        functools.partial(kernel, heads, plan(heads, chans // 128)),
        out_shape=(jax.ShapeDtypeStruct((rows, chans), bf16), jax.ShapeDtypeStruct((rows, chans), bf16)),
        in_specs=[pl.BlockSpec(memory_space=pl.ANY)] * 10,
        out_specs=[pl.BlockSpec(memory_space=pltpu.VMEM)] * 2,
        scratch_shapes=scratch,
        name="mixers",
        compiler_params=pltpu.CompilerParams(collective_id=0, has_side_effects=True, vmem_limit_bytes=60 << 20),
    )(
        hyena_q, hyena_k, hyena_v, filters, direct.reshape(chans // HD, HD), queries, keys, values,
        segment_ids.reshape(1, rows), out_weight,
    )
    half = vmem((2, rows // 2, chans), bf16)
    return pl.pallas_call(
        deliver,
        out_shape=(jax.ShapeDtypeStruct((rows, chans), bf16), jax.ShapeDtypeStruct((rows, chans), bf16)),
        in_specs=[pl.BlockSpec(memory_space=pl.ANY)] * 2,
        out_specs=[pl.BlockSpec(memory_space=pl.ANY)] * 2,
        scratch_shapes=[half, half, dma((2, 4))],
        name="deliver",
        compiler_params=pltpu.CompilerParams(vmem_limit_bytes=60 << 20),
    )(hyena_out, attn_out)


def solution(mesh):
    placed = (
        P("ctx", "tp"), P("ctx", "tp"), P("ctx", "tp"), P("tp", None), P("tp"),
        P("ctx", "tp"), P("ctx", "tp"), P("ctx", "tp"), P("ctx"), P(None, "tp"),
    )
    return jax.shard_map(
        local,
        mesh=mesh,
        in_specs=placed,
        out_specs=(P("ctx", "tp"), P("ctx", "tp")),
        check_vma=False,
    )
```

```python
import functools
import math

import jax
import jax.numpy as jnp
from jax import lax
from jax.experimental import pallas as pl
from jax.experimental.pallas import tpu as pltpu
from jax.sharding import PartitionSpec as P

HD = 128
WINDOW = 8
TAPS = 128
GROUP = 16
KEY_HOPS = 2
QUERY_HOPS = WINDOW - 1 - KEY_HOPS
NEG = -1e30
MESH = pl.DeviceIdType.MESH


ORDER = (
    ("q", 1, 1), ("k", 2, 1), ("segk", 0), ("taps",), ("vt", 0), ("k", 0, 1), ("v", 0, 1), ("k", 3, 1), ("q", 0, 1),
    ("vt", 3), ("k", 1, 1), ("vt", 2), ("local", 0, 0), ("q", 2, 1), ("vt", 1), ("v", 3, 1), ("v", 2, 1),
    ("v", 1, 1), ("q", 1, 2), ("local", 2, 0), ("q", 3, 1), ("segk", 1), ("k", 2, 2), ("q", 2, 2), ("k", 0, 2),
    ("local", 1, 0), ("q", 0, 2), ("v", 0, 2), ("q", 3, 2), ("mix",), ("k", 1, 2), ("q", 2, 3), ("q", 0, 3),
    ("q", 1, 3), ("local", 0, 1), ("v", 3, 2), ("q", 3, 3), ("local", 2, 1), ("halo", 0), ("halo", 2), ("q", 0, 4),
    ("v", 1, 2), ("halo", 3), ("q", 1, 4), ("q", 2, 4), ("q", 0, 5), ("halo", 1), ("q", 1, 5), ("segk", 2),
    ("k", 3, 2), ("v", 2, 2), ("part", 0, 1), ("part", 0, 2), ("local", 1, 1), ("q", 3, 4), ("q", 2, 5),
    ("part", 0, 4), ("part", 0, 5), ("o", 0, 5), ("part", 0, 3), ("part", 1, 1), ("part", 1, 5), ("o", 1, 5),
    ("q", 3, 5), ("o", 0, 4), ("part", 1, 4), ("part", 3, 4), ("local", 1, 2), ("o", 1, 4), ("part", 2, 5),
    ("o", 2, 5), ("hyena", 0), ("part", 3, 3), ("part", 3, 5), ("o", 3, 5), ("hyena", 5), ("part", 1, 2),
    ("o", 0, 3), ("part", 1, 3), ("o", 1, 3), ("part", 3, 1), ("part", 2, 1), ("part", 2, 4), ("o", 2, 4),
    ("o", 3, 4), ("part", 2, 3), ("hyena", 2), ("o", 0, 2), ("o", 1, 2), ("local", 0, 2), ("part", 3, 2),
    ("hyena", 3), ("o", 2, 3), ("hyena", 1), ("o", 3, 3), ("o", 0, 1), ("hyena", 7), ("o", 1, 1), ("part", 2, 2),
    ("o", 2, 2), ("o", 3, 2), ("local", 3, 0), ("local", 3, 1), ("home", 0), ("g1", 0), ("local", 2, 2),
    ("local", 3, 2), ("hyena", 4), ("g0", 0), ("home", 1), ("o", 2, 1), ("g1", 1), ("g0", 1), ("hyena", 6),
    ("o", 3, 1), ("home", 2), ("g1", 2), ("home", 3), ("g1", 3), ("g0", 3), ("g2", 1), ("g2", 0), ("proj", 1, 0),
    ("proj", 0, 0), ("g0", 2), ("proj", 0, 3), ("g2", 2), ("proj", 1, 1), ("proj", 0, 2), ("proj", 0, 1), ("g2", 3),
    ("proj", 1, 2), ("proj", 1, 3),
)


def merge(first, second):
    high_a, total_a, sum_a = first
    high_b, total_b, sum_b = second
    high = jnp.maximum(high_a, high_b)
    fade_a, fade_b = jnp.exp2(high_a - high), jnp.exp2(high_b - high)
    return high, total_a * fade_a + total_b * fade_b, sum_a * fade_a + sum_b * fade_b


def kernel(
    heads,
    order,
    hq_hbm, hk_hbm, hv_hbm, filters_hbm, direct_hbm, q_hbm, k_hbm, v_hbm, seg_hbm, w_hbm,
    hyena_hbm, attn_hbm,
    hyena_out, attn_out, hq, hk, hv, filters, direct, q_own, k_own, v_own, vt_own, seg_own, weight,
    q_in, segq_in, k_in, vt_in, segk_in, segk_col, ext, taps,
    part_sum, part_stat, out_sum, out_stat, in_sum, in_stat, local_sum, local_stat,
    attn, attn_in, total,
    load_sem, head_sem, q_sem, k_sem, v_sem, segq_sem, segk_sem, halo_sem, o_sem, ostat_sem, g_sem, out_sem,
):
    ctx, tp = lax.axis_index("ctx"), lax.axis_index("tp")
    count = lax.axis_size("ctx")
    right, left = lax.rem(ctx + 1, count), lax.rem(ctx + count - 1, count)
    mate = tp + 1 - 2 * lax.rem(tp, 2)
    across = lax.rem(tp + 2, 4)
    diagonal = lax.rem(mate + 2, 4)
    rows, chans = hk.shape
    scale = math.log2(math.e) / math.sqrt(HD)

    loads = {}

    def load(name, source, target, sem):
        loads[name] = pltpu.make_async_copy(source, target, sem)
        loads[name].start()

    for h in range(heads):
        load(("q", h), q_hbm.at[:, pl.ds(h * HD, HD)], q_own.at[h], head_sem.at[0, h])
        load(("k", h), k_hbm.at[:, pl.ds(h * HD, HD)], k_own.at[h], head_sem.at[1, h])
        load(("v", h), v_hbm.at[:, pl.ds(h * HD, HD)], v_own.at[h], head_sem.at[2, h])
    load("seg", seg_hbm, seg_own, load_sem.at[0])
    load("hk", hk_hbm, hk, load_sem.at[1])
    load("hv", hv_hbm, hv, load_sem.at[2])
    load("filters", filters_hbm, filters, load_sem.at[3])
    load("direct", direct_hbm, direct, load_sem.at[4])
    load("hq", hq_hbm, hq, load_sem.at[5])
    load("weight", w_hbm, weight, load_sem.at[6])

    done = set()
    stores = []

    def store(source, target, lanes, sem):
        stores.append(pltpu.make_async_copy(source.at[:, lanes], target.at[:, lanes], sem))
        stores[-1].start()

    def loaded(name):
        if name not in done:
            done.add(name)
            loads[name].wait()

    barrier = pltpu.get_barrier_semaphore()
    for peer in ({"ctx": left}, {"ctx": right}, {"tp": mate}, {"tp": across}):
        pl.semaphore_signal(barrier, inc=1, device_id=peer, device_id_type=MESH)
    pl.semaphore_wait(barrier, 4)

    copies = {}

    def copy(name, source, target, sems, index, peer):
        copies[name] = pltpu.make_async_remote_copy(
            src_ref=source,
            dst_ref=target,
            send_sem=sems.at[(0,) + index],
            recv_sem=sems.at[(1,) + index],
            device_id=peer,
            device_id_type=MESH,
        )

    for r in range(1, QUERY_HOPS + 1):
        for h in range(heads):
            copy(("q", h, r), q_own.at[h] if r == 1 else q_in.at[r - 2, h], q_in.at[r - 1, h], q_sem, (r - 1, h), {"ctx": left})
            copy(("o", h, r), out_sum.at[r - 1, h], in_sum.at[r - 1, h], o_sem, (r - 1, h), {"ctx": right})
            copy(("ostat", h, r), out_stat.at[r - 1, h], in_stat.at[r - 1, h], ostat_sem, (r - 1, h), {"ctx": right})
        copy(("segq", r), seg_own if r == 1 else segq_in.at[r - 2], segq_in.at[r - 1], segq_sem, (r - 1,), {"ctx": left})
    for r in range(1, KEY_HOPS + 1):
        for h in range(heads):
            copy(("k", h, r), k_own.at[h] if r == 1 else k_in.at[r - 2, h], k_in.at[r - 1, h], k_sem, (r - 1, h), {"ctx": right})
            copy(("v", h, r), vt_own.at[h] if r == 1 else vt_in.at[r - 2, h], vt_in.at[r - 1, h], v_sem, (r - 1, h), {"ctx": right})
        copy(("segk", r), seg_own if r == 1 else segk_in.at[r - 2], segk_in.at[r - 1], segk_sem, (r - 1,), {"ctx": right})
    strip = chans // heads
    for h in range(heads):
        lanes = pl.ds(h * strip, strip)
        copy(("halo", h), ext.at[pl.ds(rows, TAPS), lanes], ext.at[pl.ds(0, TAPS), lanes], halo_sem, (h,), {"ctx": right})
        half = pl.ds(h % 2 * HD, HD)
        mine = attn.at[h // 2, :, half]
        copy(("g0", h), mine, attn_in.at[0, h // 2, :, half], g_sem, (0, h), {"tp": mate})
        copy(("g1", h), mine, attn_in.at[1, h // 2, :, half], g_sem, (1, h), {"tp": across})
        copy(("g2", h), attn_in.at[1, h // 2, :, half], attn_in.at[2, h // 2, :, half], g_sem, (2, h), {"tp": mate})

    got = set()

    def arrived(name):
        if name not in got:
            got.add(name)
            copies[name].wait_recv()

    def send(name):
        copies[name].start()

    def column(row):
        return jnp.transpose(jnp.broadcast_to(row.astype(jnp.float32), (HD, rows)))

    def partial(query, query_seg, key, value_t, key_col, causal):
        score = lax.dot_general(key[...], query[...], (((1,), (1,)), ((), ())), preferred_element_type=jnp.float32)
        col = key_col[...]
        allowed = jnp.concatenate([col] * (rows // HD), axis=1) == query_seg[...].astype(jnp.float32)
        if causal:
            allowed = allowed & (
                lax.broadcasted_iota(jnp.int32, (rows, rows), 0) <= lax.broadcasted_iota(jnp.int32, (rows, rows), 1)
            )
        score = jnp.where(allowed, score * scale, NEG)
        high = jnp.max(score, axis=0, keepdims=True)
        expo = jnp.exp2(score - high)
        amount = jnp.sum(expo, axis=0, keepdims=True)
        summed = jnp.dot(value_t[...], expo.astype(jnp.bfloat16), preferred_element_type=jnp.float32)
        return high, amount, summed

    def keep(state, stat_ref, sum_ref):
        stat_ref[0:1, :] = state[0]
        stat_ref[1:2, :] = state[1]
        sum_ref[...] = state[2].astype(sum_ref.dtype)

    def fetch(stat_ref, sum_ref):
        return stat_ref[0:1, :], stat_ref[1:2, :], sum_ref[...].astype(jnp.float32)

    def step_q(h, r):
        if r == 1:
            loaded(("q", h))
            if h == 0:
                loaded("seg")
        else:
            arrived(("q", h, r - 1))
            if h == 0:
                arrived(("segq", r - 1))
        if h == 0:
            send(("segq", r))
        send(("q", h, r))

    def step_k(h, r):
        if r == 1:
            loaded(("k", h))
            if h == 0:
                loaded("seg")
        else:
            arrived(("k", h, r - 1))
            if h == 0:
                arrived(("segk", r - 1))
        if h == 0:
            send(("segk", r))
        send(("k", h, r))

    def step_vt(h):
        loaded(("v", h))
        vt_own[h] = jnp.transpose(v_own[h])

    def step_v(h, r):
        if r > 1:
            arrived(("v", h, r - 1))
        send(("v", h, r))

    def step_mix():
        loaded("hk")
        loaded("hv")
        for lo in range(0, rows, 64):
            ext[pl.ds(TAPS + lo, 64), :] = (
                hk[pl.ds(lo, 64), :].astype(jnp.float32) * hv[pl.ds(lo, 64), :].astype(jnp.float32)
            ).astype(jnp.bfloat16)

    def step_halo(h):
        send(("halo", h))

    def step_segk(d):
        if d == 0:
            loaded("seg")
            segk_col[0] = column(seg_own[...])
        else:
            arrived(("segk", d))
            segk_col[d] = column(segk_in[d - 1])

    def step_part(h, a):
        arrived(("q", h, a))
        arrived(("segq", a))
        arrived(("k", h, KEY_HOPS))
        arrived(("v", h, KEY_HOPS))
        state = partial(q_in.at[a - 1, h], segq_in.at[a - 1], k_in.at[KEY_HOPS - 1, h], vt_in.at[KEY_HOPS - 1, h], segk_col.at[KEY_HOPS], False)
        if a == QUERY_HOPS:
            keep(state, out_stat.at[a - 1, h], out_sum.at[a - 1, h])
        else:
            keep(state, part_stat.at[a - 1, h], part_sum.at[a - 1, h])

    def step_local(h, d):
        if d == 0:
            state = partial(q_own.at[h], seg_own, k_own.at[h], vt_own.at[h], segk_col.at[0], True)
        else:
            arrived(("k", h, d))
            arrived(("v", h, d))
            state = partial(q_own.at[h], seg_own, k_in.at[d - 1, h], vt_in.at[d - 1, h], segk_col.at[d], False)
            state = merge(fetch(local_stat.at[h], local_sum.at[h]), state)
        keep(state, local_stat.at[h], local_sum.at[h])

    def step_o(h, a):
        if a < QUERY_HOPS:
            arrived(("o", h, a + 1))
            arrived(("ostat", h, a + 1))
            state = merge(fetch(part_stat.at[a - 1, h], part_sum.at[a - 1, h]), fetch(in_stat.at[a, h], in_sum.at[a, h]))
            keep(state, out_stat.at[a - 1, h], out_sum.at[a - 1, h])
        send(("o", h, a))
        send(("ostat", h, a))

    def step_home(h):
        arrived(("o", h, 1))
        arrived(("ostat", h, 1))
        _, amount, summed = merge(fetch(local_stat.at[h], local_sum.at[h]), fetch(in_stat.at[0, h], in_sum.at[0, h]))
        result = jnp.transpose(summed / amount)
        attn[h // 2, :, pl.ds(h % 2 * HD, HD)] = result.astype(jnp.bfloat16)

    def step_g0(h):
        send(("g0", h))

    def step_g1(h):
        send(("g1", h))

    def step_g2(h):
        arrived(("g1", h))
        send(("g2", h))

    projected = []
    width = 256

    def step_proj(p, j):
        loaded("weight")
        if j:
            for h in (2 * p, 2 * p + 1):
                arrived((("g0", "g1", "g2")[j - 1], h))
        block = attn[p] if j == 0 else attn_in[j - 1, p]
        owner = (tp, mate, across, diagonal)[j]
        start = pl.multiple_of(owner * (heads * HD) + p * 2 * HD, 2 * HD)
        first, last = not projected, len(projected) == 2 * heads - 1
        projected.append((p, j))
        for lo in range(0, chans, width):
            lanes = pl.ds(lo, width)
            term = jnp.dot(block, weight[pl.ds(start, 2 * HD), lanes], preferred_element_type=jnp.float32)
            if not first:
                term = total[:, lanes] + term
            if last:
                attn_out[:, lanes] = term.astype(jnp.bfloat16)
                store(attn_out, attn_hbm, lanes, out_sem.at[1, lo // width])
            else:
                total[:, lanes] = term

    def step_taps():
        loaded("filters")
        tap = lax.broadcasted_iota(jnp.int32, (TAPS, 2 * TAPS), 0)
        place = lax.broadcasted_iota(jnp.int32, (TAPS, 2 * TAPS), 1)
        flip = jnp.where(tap + place == TAPS, 1.0, 0.0).astype(jnp.bfloat16)
        taps[...] = jnp.dot(filters[...], flip, preferred_element_type=jnp.float32)

    def step_hyena(c):
        if c == 0:
            for h in range(heads):
                arrived(("halo", h))
            loaded("hq")
            loaded("direct")
        lanes = pl.ds(c * 128, 128)
        before = ext[pl.ds(0, TAPS), lanes]
        before = jnp.where(ctx == 0, jnp.zeros_like(before), before)
        upper, lower = ext[pl.ds(TAPS, TAPS), lanes], ext[pl.ds(2 * TAPS, TAPS), lanes]
        data = jnp.concatenate(
            [jnp.concatenate([before, upper], axis=0), jnp.concatenate([upper, lower], axis=0)], axis=1
        )
        group = lax.rem(lax.broadcasted_iota(jnp.int32, (TAPS, 2 * TAPS), 1), 128) // GROUP
        conv = jnp.zeros((TAPS, 2 * TAPS), jnp.float32)
        per = 128 // GROUP
        for g in range(per):
            row = jnp.broadcast_to(taps[pl.ds(c * per + g, 1), :], (TAPS, 2 * TAPS))
            table = pltpu.roll(row, 0, 1, stride=1, stride_axis=0).astype(jnp.bfloat16)
            conv = jnp.where(group == g, jnp.dot(table, data, preferred_element_type=jnp.float32), conv)
        gain = direct[...].astype(jnp.float32)[c : c + 1, :]
        for b, mixed in enumerate((upper, lower)):
            span = pl.ds(b * TAPS, TAPS)
            hyena_out[span, lanes] = (
                hq[span, lanes].astype(jnp.float32)
                * (conv[:, b * TAPS : (b + 1) * TAPS] + gain * mixed.astype(jnp.float32))
            ).astype(jnp.bfloat16)
        store(hyena_out, hyena_hbm, lanes, out_sem.at[0, c])

    steps = dict(
        q=step_q, k=step_k, vt=step_vt, v=step_v, mix=step_mix, halo=step_halo, segk=step_segk, part=step_part,
        local=step_local, o=step_o, home=step_home, g0=step_g0, g1=step_g1, g2=step_g2, proj=step_proj,
        taps=step_taps, hyena=step_hyena,
    )
    for name in order:
        steps[name[0]](*name[1:])
    for name in copies:
        arrived(name)
        copies[name].wait_send()
    for move in stores:
        move.wait()


def deliver(hyena_ref, attn_ref, hyena_out, attn_out, hyena_buf, attn_buf, sems):
    size = hyena_buf.shape[1]
    loads, stores = [], []
    for i, (source, target, buf) in enumerate(((hyena_ref, hyena_out, hyena_buf), (attn_ref, attn_out, attn_buf))):
        for j in range(2):
            span = pl.ds(j * size, size)
            loads.append(pltpu.make_async_copy(source.at[span, :], buf.at[j], sems.at[0, 2 * i + j]))
            stores.append(pltpu.make_async_copy(buf.at[j], target.at[span, :], sems.at[1, 2 * i + j]))
    for move in loads:
        move.start()
    for move, store in zip(loads, stores):
        move.wait()
        store.start()
    for store in stores:
        store.wait()


def local(hyena_q, hyena_k, hyena_v, filters, direct, queries, keys, values, segment_ids, out_weight):
    rows, feat = queries.shape
    chans = hyena_k.shape[1]
    heads = feat // HD
    groups = filters.shape[0]
    depth = out_weight.shape[0]
    bf16, f32, i32 = jnp.bfloat16, jnp.float32, jnp.int32
    dma = pltpu.SemaphoreType.DMA
    vmem = pltpu.VMEM
    scratch = [
        vmem((rows, chans), bf16), vmem((rows, chans), bf16),
        vmem((rows, chans), bf16), vmem((rows, chans), bf16), vmem((rows, chans), bf16),
        vmem((groups, TAPS), bf16), vmem((chans // HD, HD), bf16),
        vmem((heads, rows, HD), bf16), vmem((heads, rows, HD), bf16), vmem((heads, rows, HD), bf16),
        vmem((heads, HD, rows), bf16), vmem((1, rows), i32), vmem((depth, chans), bf16),
        vmem((QUERY_HOPS, heads, rows, HD), bf16), vmem((QUERY_HOPS, 1, rows), i32),
        vmem((KEY_HOPS, heads, rows, HD), bf16), vmem((KEY_HOPS, heads, HD, rows), bf16), vmem((KEY_HOPS, 1, rows), i32),
        vmem((KEY_HOPS + 1, rows, HD), f32), vmem((TAPS + rows, chans), bf16), vmem((groups, 2 * TAPS), f32),
        vmem((QUERY_HOPS, heads, HD, rows), f32), vmem((QUERY_HOPS, heads, 2, rows), f32),
        vmem((QUERY_HOPS, heads, HD, rows), bf16), vmem((QUERY_HOPS, heads, 2, rows), f32),
        vmem((QUERY_HOPS, heads, HD, rows), bf16), vmem((QUERY_HOPS, heads, 2, rows), f32),
        vmem((heads, HD, rows), f32), vmem((heads, 2, rows), f32),
        vmem((heads // 2, rows, 2 * HD), bf16), vmem((3, heads // 2, rows, 2 * HD), bf16), vmem((rows, chans), f32),
        dma((7,)), dma((3, heads)), dma((2, QUERY_HOPS, heads)), dma((2, KEY_HOPS, heads)), dma((2, KEY_HOPS, heads)),
        dma((2, QUERY_HOPS)), dma((2, KEY_HOPS)), dma((2, heads)), dma((2, QUERY_HOPS, heads)), dma((2, QUERY_HOPS, heads)),
        dma((2, 3, heads)), dma((2, chans // HD)),
    ]
    hyena_out, attn_out = pl.pallas_call(
        functools.partial(kernel, heads, ORDER),
        out_shape=(jax.ShapeDtypeStruct((rows, chans), bf16), jax.ShapeDtypeStruct((rows, chans), bf16)),
        in_specs=[pl.BlockSpec(memory_space=pl.ANY)] * 10,
        out_specs=[pl.BlockSpec(memory_space=pl.ANY)] * 2,
        scratch_shapes=scratch,
        name="mixers",
        compiler_params=pltpu.CompilerParams(collective_id=0, has_side_effects=True, vmem_limit_bytes=60 << 20),
    )(
        hyena_q, hyena_k, hyena_v, filters, direct.reshape(chans // HD, HD), queries, keys, values,
        segment_ids.reshape(1, rows), out_weight,
    )
    half = vmem((2, rows // 2, chans), bf16)
    return pl.pallas_call(
        deliver,
        out_shape=(jax.ShapeDtypeStruct((rows, chans), bf16), jax.ShapeDtypeStruct((rows, chans), bf16)),
        in_specs=[pl.BlockSpec(memory_space=pl.ANY)] * 2,
        out_specs=[pl.BlockSpec(memory_space=pl.ANY)] * 2,
        scratch_shapes=[half, half, dma((2, 4))],
        name="deliver",
        compiler_params=pltpu.CompilerParams(vmem_limit_bytes=60 << 20),
    )(hyena_out, attn_out)


def solution(mesh):
    placed = (
        P("ctx", "tp"), P("ctx", "tp"), P("ctx", "tp"), P("tp", None), P("tp"),
        P("ctx", "tp"), P("ctx", "tp"), P("ctx", "tp"), P("ctx"), P(None, "tp"),
    )
    return jax.shard_map(
        local,
        mesh=mesh,
        in_specs=placed,
        out_specs=(P("ctx", "tp"), P("ctx", "tp")),
        check_vma=False,
    )
```

```python
import functools
import math

import jax
import jax.numpy as jnp
from jax import lax
from jax.experimental import pallas as pl
from jax.experimental.pallas import tpu as pltpu
from jax.sharding import PartitionSpec as P

HD = 128
WINDOW = 8
TAPS = 128
GROUP = 16
KEY_HOPS = 2
QUERY_HOPS = WINDOW - 1 - KEY_HOPS
NEG = -1e30
MESH = pl.DeviceIdType.MESH


ORDER = (
    ("q", 1, 1), ("k", 2, 1), ("segk", 0), ("taps",), ("vt", 0), ("k", 0, 1), ("v", 0, 1), ("k", 3, 1), ("q", 0, 1),
    ("vt", 3), ("k", 1, 1), ("vt", 2), ("local", 0, 0), ("q", 2, 1), ("vt", 1), ("v", 3, 1), ("v", 2, 1),
    ("v", 1, 1), ("q", 1, 2), ("local", 2, 0), ("q", 3, 1), ("segk", 1), ("k", 2, 2), ("q", 2, 2), ("k", 0, 2),
    ("local", 1, 0), ("q", 0, 2), ("v", 0, 2), ("q", 3, 2), ("mix",), ("k", 1, 2), ("q", 2, 3), ("q", 0, 3),
    ("q", 1, 3), ("local", 0, 1), ("v", 3, 2), ("q", 3, 3), ("local", 2, 1), ("halo", 0), ("halo", 2), ("q", 0, 4),
    ("v", 1, 2), ("halo", 3), ("q", 1, 4), ("q", 2, 4), ("q", 0, 5), ("halo", 1), ("q", 1, 5), ("segk", 2),
    ("k", 3, 2), ("v", 2, 2), ("part", 0, 1), ("part", 0, 2), ("local", 1, 1), ("q", 3, 4), ("q", 2, 5),
    ("part", 0, 4), ("part", 0, 5), ("o", 0, 5), ("part", 0, 3), ("part", 1, 1), ("part", 1, 5), ("o", 1, 5),
    ("q", 3, 5), ("o", 0, 4), ("part", 1, 4), ("part", 3, 4), ("local", 1, 2), ("o", 1, 4), ("part", 2, 5),
    ("o", 2, 5), ("hyena", 0), ("part", 3, 3), ("part", 3, 5), ("o", 3, 5), ("hyena", 5), ("part", 1, 2),
    ("o", 0, 3), ("part", 1, 3), ("o", 1, 3), ("part", 3, 1), ("part", 2, 1), ("part", 2, 4), ("o", 2, 4),
    ("o", 3, 4), ("part", 2, 3), ("hyena", 2), ("o", 0, 2), ("o", 1, 2), ("local", 0, 2), ("part", 3, 2),
    ("hyena", 3), ("o", 2, 3), ("hyena", 1), ("o", 3, 3), ("o", 0, 1), ("hyena", 7), ("o", 1, 1), ("part", 2, 2),
    ("o", 2, 2), ("o", 3, 2), ("local", 3, 0), ("local", 3, 1), ("home", 0), ("g1", 0), ("local", 2, 2),
    ("local", 3, 2), ("hyena", 4), ("g0", 0), ("home", 1), ("o", 2, 1), ("g1", 1), ("g0", 1), ("hyena", 6),
    ("o", 3, 1), ("home", 2), ("g1", 2), ("home", 3), ("g1", 3), ("g0", 3), ("g2", 1), ("g2", 0), ("proj", 1, 0),
    ("proj", 0, 0), ("g0", 2), ("proj", 0, 3), ("g2", 2), ("proj", 1, 1), ("proj", 0, 2), ("proj", 0, 1), ("g2", 3),
    ("proj", 1, 2), ("proj", 1, 3),
)


def merge(first, second):
    high_a, total_a, sum_a = first
    high_b, total_b, sum_b = second
    high = jnp.maximum(high_a, high_b)
    fade_a, fade_b = jnp.exp2(high_a - high), jnp.exp2(high_b - high)
    return high, total_a * fade_a + total_b * fade_b, sum_a * fade_a + sum_b * fade_b


def kernel(
    heads,
    order,
    hq_hbm, hk_hbm, hv_hbm, filters_hbm, direct_hbm, q_hbm, k_hbm, v_hbm, seg_hbm, w_hbm,
    hyena_hbm, attn_hbm,
    hyena_out, attn_out, hq, hk, hv, filters, direct, q_own, k_own, v_own, vt_own, seg_own, weight,
    q_in, segq_in, k_in, vt_in, segk_in, segk_col, ext, taps,
    part_sum, part_stat, out_sum, out_stat, in_sum, in_stat, local_sum, local_stat,
    attn, attn_in, total,
    load_sem, head_sem, q_sem, k_sem, v_sem, segq_sem, segk_sem, halo_sem, o_sem, ostat_sem, g_sem, out_sem,
):
    ctx, tp = lax.axis_index("ctx"), lax.axis_index("tp")
    count = lax.axis_size("ctx")
    right, left = lax.rem(ctx + 1, count), lax.rem(ctx + count - 1, count)
    mate = tp + 1 - 2 * lax.rem(tp, 2)
    across = lax.rem(tp + 2, 4)
    diagonal = lax.rem(mate + 2, 4)
    rows, chans = hk.shape
    scale = math.log2(math.e) / math.sqrt(HD)

    barrier = pltpu.get_barrier_semaphore()
    for peer in ({"ctx": left}, {"ctx": right}, {"tp": mate}, {"tp": across}):
        pl.semaphore_signal(barrier, inc=1, device_id=peer, device_id_type=MESH)

    loads = {}

    def load(name, source, target, sem):
        loads[name] = pltpu.make_async_copy(source, target, sem)
        loads[name].start()

    for h in range(heads):
        load(("q", h), q_hbm.at[:, pl.ds(h * HD, HD)], q_own.at[h], head_sem.at[0, h])
        load(("k", h), k_hbm.at[:, pl.ds(h * HD, HD)], k_own.at[h], head_sem.at[1, h])
        load(("v", h), v_hbm.at[:, pl.ds(h * HD, HD)], v_own.at[h], head_sem.at[2, h])
    load("seg", seg_hbm, seg_own, load_sem.at[0])
    load("hk", hk_hbm, hk, load_sem.at[1])
    load("hv", hv_hbm, hv, load_sem.at[2])
    load("filters", filters_hbm, filters, load_sem.at[3])
    load("direct", direct_hbm, direct, load_sem.at[4])
    load("hq", hq_hbm, hq, load_sem.at[5])
    load("weight", w_hbm, weight, load_sem.at[6])

    done = set()
    stores = []

    def store(source, target, lanes, sem):
        stores.append(pltpu.make_async_copy(source.at[:, lanes], target.at[:, lanes], sem))
        stores[-1].start()

    def loaded(name):
        if name not in done:
            done.add(name)
            loads[name].wait()

    pl.semaphore_wait(barrier, 4)

    copies = {}

    def copy(name, source, target, sems, index, peer):
        copies[name] = pltpu.make_async_remote_copy(
            src_ref=source,
            dst_ref=target,
            send_sem=sems.at[(0,) + index],
            recv_sem=sems.at[(1,) + index],
            device_id=peer,
            device_id_type=MESH,
        )

    for r in range(1, QUERY_HOPS + 1):
        for h in range(heads):
            copy(("q", h, r), q_own.at[h] if r == 1 else q_in.at[r - 2, h], q_in.at[r - 1, h], q_sem, (r - 1, h), {"ctx": left})
            copy(("o", h, r), out_sum.at[r - 1, h], in_sum.at[r - 1, h], o_sem, (r - 1, h), {"ctx": right})
            copy(("ostat", h, r), out_stat.at[r - 1, h], in_stat.at[r - 1, h], ostat_sem, (r - 1, h), {"ctx": right})
        copy(("segq", r), seg_own if r == 1 else segq_in.at[r - 2], segq_in.at[r - 1], segq_sem, (r - 1,), {"ctx": left})
    for r in range(1, KEY_HOPS + 1):
        for h in range(heads):
            copy(("k", h, r), k_own.at[h] if r == 1 else k_in.at[r - 2, h], k_in.at[r - 1, h], k_sem, (r - 1, h), {"ctx": right})
            copy(("v", h, r), vt_own.at[h] if r == 1 else vt_in.at[r - 2, h], vt_in.at[r - 1, h], v_sem, (r - 1, h), {"ctx": right})
        copy(("segk", r), seg_own if r == 1 else segk_in.at[r - 2], segk_in.at[r - 1], segk_sem, (r - 1,), {"ctx": right})
    strip = chans // heads
    for h in range(heads):
        lanes = pl.ds(h * strip, strip)
        copy(("halo", h), ext.at[pl.ds(rows, TAPS), lanes], ext.at[pl.ds(0, TAPS), lanes], halo_sem, (h,), {"ctx": right})
        half = pl.ds(h % 2 * HD, HD)
        mine = attn.at[h // 2, :, half]
        copy(("g0", h), mine, attn_in.at[0, h // 2, :, half], g_sem, (0, h), {"tp": mate})
        copy(("g1", h), mine, attn_in.at[1, h // 2, :, half], g_sem, (1, h), {"tp": across})
        copy(("g2", h), attn_in.at[1, h // 2, :, half], attn_in.at[2, h // 2, :, half], g_sem, (2, h), {"tp": mate})

    got = set()

    def arrived(name):
        if name not in got:
            got.add(name)
            copies[name].wait_recv()

    def send(name):
        copies[name].start()

    def column(row):
        return jnp.transpose(jnp.broadcast_to(row.astype(jnp.float32), (HD, rows)))

    def partial(query, query_seg, key, value_t, key_col, causal):
        score = lax.dot_general(key[...], query[...], (((1,), (1,)), ((), ())), preferred_element_type=jnp.float32)
        col = key_col[...]
        allowed = jnp.concatenate([col] * (rows // HD), axis=1) == query_seg[...].astype(jnp.float32)
        if causal:
            allowed = allowed & (
                lax.broadcasted_iota(jnp.int32, (rows, rows), 0) <= lax.broadcasted_iota(jnp.int32, (rows, rows), 1)
            )
        score = jnp.where(allowed, score * scale, NEG)
        high = jnp.max(score, axis=0, keepdims=True)
        expo = jnp.exp2(score - high)
        amount = jnp.sum(expo, axis=0, keepdims=True)
        summed = jnp.dot(value_t[...], expo.astype(jnp.bfloat16), preferred_element_type=jnp.float32)
        return high, amount, summed

    def keep(state, stat_ref, sum_ref):
        stat_ref[0:1, :] = state[0]
        stat_ref[1:2, :] = state[1]
        sum_ref[...] = state[2].astype(sum_ref.dtype)

    def fetch(stat_ref, sum_ref):
        return stat_ref[0:1, :], stat_ref[1:2, :], sum_ref[...].astype(jnp.float32)

    def step_q(h, r):
        if r == 1:
            loaded(("q", h))
            if h == 0:
                loaded("seg")
        else:
            arrived(("q", h, r - 1))
            if h == 0:
                arrived(("segq", r - 1))
        if h == 0:
            send(("segq", r))
        send(("q", h, r))

    def step_k(h, r):
        if r == 1:
            loaded(("k", h))
            if h == 0:
                loaded("seg")
        else:
            arrived(("k", h, r - 1))
            if h == 0:
                arrived(("segk", r - 1))
        if h == 0:
            send(("segk", r))
        send(("k", h, r))

    def step_vt(h):
        loaded(("v", h))
        vt_own[h] = jnp.transpose(v_own[h])

    def step_v(h, r):
        if r > 1:
            arrived(("v", h, r - 1))
        send(("v", h, r))

    def step_mix():
        loaded("hk")
        loaded("hv")
        for lo in range(0, rows, 64):
            ext[pl.ds(TAPS + lo, 64), :] = (
                hk[pl.ds(lo, 64), :].astype(jnp.float32) * hv[pl.ds(lo, 64), :].astype(jnp.float32)
            ).astype(jnp.bfloat16)

    def step_halo(h):
        send(("halo", h))

    def step_segk(d):
        if d == 0:
            loaded("seg")
            segk_col[0] = column(seg_own[...])
        else:
            arrived(("segk", d))
            segk_col[d] = column(segk_in[d - 1])

    def step_part(h, a):
        arrived(("q", h, a))
        arrived(("segq", a))
        arrived(("k", h, KEY_HOPS))
        arrived(("v", h, KEY_HOPS))
        state = partial(q_in.at[a - 1, h], segq_in.at[a - 1], k_in.at[KEY_HOPS - 1, h], vt_in.at[KEY_HOPS - 1, h], segk_col.at[KEY_HOPS], False)
        if a == QUERY_HOPS:
            keep(state, out_stat.at[a - 1, h], out_sum.at[a - 1, h])
        else:
            keep(state, part_stat.at[a - 1, h], part_sum.at[a - 1, h])

    def step_local(h, d):
        if d == 0:
            state = partial(q_own.at[h], seg_own, k_own.at[h], vt_own.at[h], segk_col.at[0], True)
        else:
            arrived(("k", h, d))
            arrived(("v", h, d))
            state = partial(q_own.at[h], seg_own, k_in.at[d - 1, h], vt_in.at[d - 1, h], segk_col.at[d], False)
            state = merge(fetch(local_stat.at[h], local_sum.at[h]), state)
        keep(state, local_stat.at[h], local_sum.at[h])

    def step_o(h, a):
        if a < QUERY_HOPS:
            arrived(("o", h, a + 1))
            arrived(("ostat", h, a + 1))
            state = merge(fetch(part_stat.at[a - 1, h], part_sum.at[a - 1, h]), fetch(in_stat.at[a, h], in_sum.at[a, h]))
            keep(state, out_stat.at[a - 1, h], out_sum.at[a - 1, h])
        send(("o", h, a))
        send(("ostat", h, a))

    def step_home(h):
        arrived(("o", h, 1))
        arrived(("ostat", h, 1))
        _, amount, summed = merge(fetch(local_stat.at[h], local_sum.at[h]), fetch(in_stat.at[0, h], in_sum.at[0, h]))
        result = jnp.transpose(summed / amount)
        attn[h // 2, :, pl.ds(h % 2 * HD, HD)] = result.astype(jnp.bfloat16)

    def step_g0(h):
        send(("g0", h))

    def step_g1(h):
        send(("g1", h))

    def step_g2(h):
        arrived(("g1", h))
        send(("g2", h))

    projected = []
    width = 256

    def step_proj(p, j):
        loaded("weight")
        if j:
            for h in (2 * p, 2 * p + 1):
                arrived((("g0", "g1", "g2")[j - 1], h))
        block = attn[p] if j == 0 else attn_in[j - 1, p]
        owner = (tp, mate, across, diagonal)[j]
        start = pl.multiple_of(owner * (heads * HD) + p * 2 * HD, 2 * HD)
        first, last = not projected, len(projected) == 2 * heads - 1
        projected.append((p, j))
        for lo in range(0, chans, width):
            lanes = pl.ds(lo, width)
            term = jnp.dot(block, weight[pl.ds(start, 2 * HD), lanes], preferred_element_type=jnp.float32)
            if not first:
                term = total[:, lanes] + term
            if last:
                attn_out[:, lanes] = term.astype(jnp.bfloat16)
                store(attn_out, attn_hbm, lanes, out_sem.at[1, lo // width])
            else:
                total[:, lanes] = term

    def step_taps():
        loaded("filters")
        tap = lax.broadcasted_iota(jnp.int32, (TAPS, 2 * TAPS), 0)
        place = lax.broadcasted_iota(jnp.int32, (TAPS, 2 * TAPS), 1)
        flip = jnp.where(tap + place == TAPS, 1.0, 0.0).astype(jnp.bfloat16)
        taps[...] = jnp.dot(filters[...], flip, preferred_element_type=jnp.float32)

    def step_hyena(c):
        if c == 0:
            for h in range(heads):
                arrived(("halo", h))
            loaded("hq")
            loaded("direct")
        lanes = pl.ds(c * 128, 128)
        before = ext[pl.ds(0, TAPS), lanes]
        before = jnp.where(ctx == 0, jnp.zeros_like(before), before)
        upper, lower = ext[pl.ds(TAPS, TAPS), lanes], ext[pl.ds(2 * TAPS, TAPS), lanes]
        data = jnp.concatenate(
            [jnp.concatenate([before, upper], axis=0), jnp.concatenate([upper, lower], axis=0)], axis=1
        )
        group = lax.rem(lax.broadcasted_iota(jnp.int32, (TAPS, 2 * TAPS), 1), 128) // GROUP
        conv = jnp.zeros((TAPS, 2 * TAPS), jnp.float32)
        per = 128 // GROUP
        for g in range(per):
            row = jnp.broadcast_to(taps[pl.ds(c * per + g, 1), :], (TAPS, 2 * TAPS))
            table = pltpu.roll(row, 0, 1, stride=1, stride_axis=0).astype(jnp.bfloat16)
            conv = jnp.where(group == g, jnp.dot(table, data, preferred_element_type=jnp.float32), conv)
        gain = direct[...].astype(jnp.float32)[c : c + 1, :]
        for b, mixed in enumerate((upper, lower)):
            span = pl.ds(b * TAPS, TAPS)
            hyena_out[span, lanes] = (
                hq[span, lanes].astype(jnp.float32)
                * (conv[:, b * TAPS : (b + 1) * TAPS] + gain * mixed.astype(jnp.float32))
            ).astype(jnp.bfloat16)
        store(hyena_out, hyena_hbm, lanes, out_sem.at[0, c])

    steps = dict(
        q=step_q, k=step_k, vt=step_vt, v=step_v, mix=step_mix, halo=step_halo, segk=step_segk, part=step_part,
        local=step_local, o=step_o, home=step_home, g0=step_g0, g1=step_g1, g2=step_g2, proj=step_proj,
        taps=step_taps, hyena=step_hyena,
    )
    for name in order:
        steps[name[0]](*name[1:])
    for name in copies:
        arrived(name)
        copies[name].wait_send()
    for move in stores:
        move.wait()


def deliver(hyena_ref, attn_ref, hyena_out, attn_out, hyena_buf, attn_buf, sems):
    size = hyena_buf.shape[1]
    loads, stores = [], []
    for i, (source, target, buf) in enumerate(((hyena_ref, hyena_out, hyena_buf), (attn_ref, attn_out, attn_buf))):
        for j in range(2):
            span = pl.ds(j * size, size)
            loads.append(pltpu.make_async_copy(source.at[span, :], buf.at[j], sems.at[0, 2 * i + j]))
            stores.append(pltpu.make_async_copy(buf.at[j], target.at[span, :], sems.at[1, 2 * i + j]))
    for move in loads:
        move.start()
    for move, store in zip(loads, stores):
        move.wait()
        store.start()
    for store in stores:
        store.wait()


def local(hyena_q, hyena_k, hyena_v, filters, direct, queries, keys, values, segment_ids, out_weight):
    rows, feat = queries.shape
    chans = hyena_k.shape[1]
    heads = feat // HD
    groups = filters.shape[0]
    depth = out_weight.shape[0]
    bf16, f32, i32 = jnp.bfloat16, jnp.float32, jnp.int32
    dma = pltpu.SemaphoreType.DMA
    vmem = pltpu.VMEM
    scratch = [
        vmem((rows, chans), bf16), vmem((rows, chans), bf16),
        vmem((rows, chans), bf16), vmem((rows, chans), bf16), vmem((rows, chans), bf16),
        vmem((groups, TAPS), bf16), vmem((chans // HD, HD), bf16),
        vmem((heads, rows, HD), bf16), vmem((heads, rows, HD), bf16), vmem((heads, rows, HD), bf16),
        vmem((heads, HD, rows), bf16), vmem((1, rows), i32), vmem((depth, chans), bf16),
        vmem((QUERY_HOPS, heads, rows, HD), bf16), vmem((QUERY_HOPS, 1, rows), i32),
        vmem((KEY_HOPS, heads, rows, HD), bf16), vmem((KEY_HOPS, heads, HD, rows), bf16), vmem((KEY_HOPS, 1, rows), i32),
        vmem((KEY_HOPS + 1, rows, HD), f32), vmem((TAPS + rows, chans), bf16), vmem((groups, 2 * TAPS), f32),
        vmem((QUERY_HOPS, heads, HD, rows), f32), vmem((QUERY_HOPS, heads, 2, rows), f32),
        vmem((QUERY_HOPS, heads, HD, rows), bf16), vmem((QUERY_HOPS, heads, 2, rows), f32),
        vmem((QUERY_HOPS, heads, HD, rows), bf16), vmem((QUERY_HOPS, heads, 2, rows), f32),
        vmem((heads, HD, rows), f32), vmem((heads, 2, rows), f32),
        vmem((heads // 2, rows, 2 * HD), bf16), vmem((3, heads // 2, rows, 2 * HD), bf16), vmem((rows, chans), f32),
        dma((7,)), dma((3, heads)), dma((2, QUERY_HOPS, heads)), dma((2, KEY_HOPS, heads)), dma((2, KEY_HOPS, heads)),
        dma((2, QUERY_HOPS)), dma((2, KEY_HOPS)), dma((2, heads)), dma((2, QUERY_HOPS, heads)), dma((2, QUERY_HOPS, heads)),
        dma((2, 3, heads)), dma((2, chans // HD)),
    ]
    hyena_out, attn_out = pl.pallas_call(
        functools.partial(kernel, heads, ORDER),
        out_shape=(jax.ShapeDtypeStruct((rows, chans), bf16), jax.ShapeDtypeStruct((rows, chans), bf16)),
        in_specs=[pl.BlockSpec(memory_space=pl.ANY)] * 10,
        out_specs=[pl.BlockSpec(memory_space=pl.ANY)] * 2,
        scratch_shapes=scratch,
        name="mixers",
        compiler_params=pltpu.CompilerParams(collective_id=0, has_side_effects=True, vmem_limit_bytes=60 << 20),
    )(
        hyena_q, hyena_k, hyena_v, filters, direct.reshape(chans // HD, HD), queries, keys, values,
        segment_ids.reshape(1, rows), out_weight,
    )
    half = vmem((2, rows // 2, chans), bf16)
    return pl.pallas_call(
        deliver,
        out_shape=(jax.ShapeDtypeStruct((rows, chans), bf16), jax.ShapeDtypeStruct((rows, chans), bf16)),
        in_specs=[pl.BlockSpec(memory_space=pl.ANY)] * 2,
        out_specs=[pl.BlockSpec(memory_space=pl.ANY)] * 2,
        scratch_shapes=[half, half, dma((2, 4))],
        name="deliver",
        compiler_params=pltpu.CompilerParams(vmem_limit_bytes=60 << 20),
    )(hyena_out, attn_out)


def solution(mesh):
    placed = (
        P("ctx", "tp"), P("ctx", "tp"), P("ctx", "tp"), P("tp", None), P("tp"),
        P("ctx", "tp"), P("ctx", "tp"), P("ctx", "tp"), P("ctx"), P(None, "tp"),
    )
    return jax.shard_map(
        local,
        mesh=mesh,
        in_specs=placed,
        out_specs=(P("ctx", "tp"), P("ctx", "tp")),
        check_vma=False,
    )
```
